32 devices in a mesh: groups: 2 (over x), seq: 4 (over y, core), chan: 4 (over z).
Axes of the slice: x: 2, y: 2, z: 4, core: 2. Of those that a mesh axis runs over, the one named last changes fastest.
Arguments:
- dna_act: bfloat16 [6, 2048, 1280], P('groups', 'seq', 'chan'), parts along dimension 0, may hold values from -5 to 5
- conv_weight: bfloat16 [5, 1280, 1536], P(None, 'chan'), may hold values from -0.078125 to 0.078125
- head_weight: bfloat16 [7611, 1536], P(None, 'chan'), may hold values from -0.078125 to 0.078125
- track_ids: int32 [1024], P('groups'), parts along dimension 0, may hold values from 0 to 7610, as said below
- bin_mask: int32 [6, 1024], P('groups', ('seq', 'chan')), parts along dimension 0, may hold values 0 or 1
- counts: int32 [6, 1024, 512], P('groups', ('seq', 'chan')), parts along dimension 0, may hold values from 0 to 3
Outputs:
- grad_input: bfloat16 [6, 2048, 1280], P('groups', 'seq', 'chan'), parts along dimension 0
- grad_conv: float32 [10, 1280, 1536], P('groups', 'chan', 'seq'), parts along dimension 0
- grad_tracks: float32 [1024, 1536], P(('groups', 'seq'), 'chan'), parts along dimension 0
The draws below stay inside these ranges and needn't reach their ends.
There are 2 independent parts, one for each index of `groups`. The reference program is written for one: setup_inputs(seed, part) draws one part's arguments, and reference() takes and returns one part's arrays. A program takes and returns all parts, laid end to end along the dimension named above; an argument that names none is the same for every part. Nothing has to cross between parts.
Inputs may be any that keep to these rules, and one draw needn't show every extreme that they name: `track_ids`: the 512 track numbers are distinct.
All inputs are finite; a program needn't handle non-finite values. No bound on the sum of `bin_mask` on one device may be relied on, other than what follows from the above.
Results may differ from the reference program's by a relative error of at most 0.011.
Values may be sent and summed in bfloat16 or wider, within the bound.
No kernel may reach another device: no remote copies, remote signals or barrier semaphores. Data moves between devices by JAX's collectives and lax.ppermute only.
A program may use at most 128 MiB of HBM per device.

```python
import jax
import jax.numpy as jnp

D = 1536
CIN = 1280
TRACKS = 7611
KSIZE = 5
SEQS = 3
MASKED = 512
LEN = 2048
BINS = 1024


def draw_track_ids(key, part):
    shuffled = jax.random.permutation(key, TRACKS)
    return shuffled[:MASKED].astype(jnp.int32)


def set_ends(result, rng, low, high):
    longest = result.shape.index(max(result.shape))
    spots = []
    for shift in (0, 1):
        where = [jax.random.randint(jax.random.fold_in(rng, axis), (), 0, length) for axis, length in enumerate(result.shape)]
        where[longest] = (where[longest] + shift) % result.shape[longest]
        spots.append(tuple(where))
    return result.at[spots[0]].set(low).at[spots[1]].set(high)


def shard_levels(rng, extent, shards, least, top_value):
    def one(position, parts):
        steps = jax.random.uniform(jax.random.fold_in(jax.random.fold_in(rng, 6), position), (parts,), jnp.float32, least / len(shards), top_value / len(shards))
        return jnp.repeat(jnp.exp(steps), extent[position] // parts).reshape((-1,) + (1,) * (len(extent) - position - 1))

    gain = one(*shards[0])
    for cut in shards[1:]:
        gain = gain * one(*cut)
    return gain


def gaussian(rng, shape, deviation, bound, split=(), kind=jnp.bfloat16):
    factor_of = shard_levels(rng, shape, split, -0.22, 0.18) if split else 1.0
    result = jax.random.normal(rng, shape, jnp.float32) * deviation * factor_of
    return jnp.minimum(jnp.maximum(result, -bound), bound).astype(kind)


def setup_inputs(seed: int = 0, part: int = 0) -> dict:
    streams_of = jax.random.split(jax.random.key(seed), 7)
    part_keys = jax.random.split(jax.random.fold_in(streams_of[6], part), 7)
    dna_act = gaussian(part_keys[0], (SEQS, LEN, CIN), 1.0, 5.0, ((1, 4), (2, 4)))
    conv_weight = gaussian(streams_of[1], (KSIZE, CIN, D), (KSIZE * CIN) ** -0.5, 0.078125, ((1, 4),))
    head_weight = gaussian(streams_of[2], (TRACKS, D), (4 * D) ** -0.5, 0.078125, ((1, 4),))
    track_ids = draw_track_ids(jax.random.fold_in(jax.random.fold_in(streams_of[6], part), 71), part)
    bin_mask = set_ends((jax.random.randint(part_keys[4], (SEQS, BINS), 0, 8) < 7).astype(jnp.int32), jax.random.fold_in(part_keys[4], 1), 0, 1)
    counts = set_ends(jax.random.randint(part_keys[5], (SEQS, BINS, MASKED), 0, 4), jax.random.fold_in(part_keys[5], 1), 0, 3).astype(jnp.int32)
    return {"dna_act": dna_act, "conv_weight": conv_weight, "head_weight": head_weight, "track_ids": track_ids, "bin_mask": bin_mask, "counts": counts}


def exact_gelu(values):
    return jax.nn.gelu(values, approximate=False)

def reference(dna_act, conv_weight, head_weight, track_ids, bin_mask, counts):
    gelu_out, gelu_back = jax.vjp(exact_gelu, dna_act.astype(jnp.float32))
    activated = gelu_out.astype(jnp.bfloat16)
    padded = jnp.pad(activated, ((0, 0), (2, 2), (0, 0)))
    conv_out = jnp.zeros((SEQS * LEN, D), jnp.float32)
    for offset in range(KSIZE):
        window = padded[:, offset:offset + LEN].reshape(SEQS * LEN, CIN)
        conv_out = conv_out + jnp.dot(window, conv_weight[offset], preferred_element_type=jnp.float32)
    pooled = (conv_out.reshape(SEQS * BINS, 2, D).sum(axis=1) * 0.5).astype(jnp.bfloat16)
    chosen = jnp.take(head_weight, track_ids, axis=0)
    logits = jnp.dot(pooled, chosen.T, preferred_element_type=jnp.float32)
    mask_column = bin_mask.reshape(SEQS * BINS, 1).astype(jnp.float32)
    targets = counts.reshape(SEQS * BINS, MASKED).astype(jnp.float32)
    grad_logit = (mask_column * (jnp.exp(logits) - targets)).astype(jnp.bfloat16)
    grad_bins = jnp.dot(grad_logit, chosen, preferred_element_type=jnp.float32).astype(jnp.bfloat16)
    grad_tracks = jnp.dot(grad_logit.T, pooled, preferred_element_type=jnp.float32)
    grad_conv_out = jnp.repeat(grad_bins.reshape(SEQS, BINS, D), 2, axis=1) * 0.5
    grad_padded = jnp.pad(grad_conv_out, ((0, 0), (2, 2), (0, 0)))
    grad_acts = jnp.zeros((SEQS * LEN, CIN), jnp.float32)
    for offset in range(KSIZE):
        window = grad_padded[:, 4 - offset:4 - offset + LEN].reshape(SEQS * LEN, D)
        grad_acts = grad_acts + jnp.dot(window, conv_weight[offset].T, preferred_element_type=jnp.float32)
    grad_input = gelu_back(grad_acts.reshape(SEQS, LEN, CIN))[0].astype(jnp.bfloat16)
    flat_grad = grad_conv_out.reshape(SEQS * LEN, D)
    filter_terms = []
    for offset in range(KSIZE):
        window = padded[:, offset:offset + LEN].reshape(SEQS * LEN, CIN)
        filter_terms.append(jnp.dot(window.T, flat_grad, preferred_element_type=jnp.float32))
    grad_conv = jnp.stack(filter_terms)
    return (grad_input, grad_conv, grad_tracks)
```

```python
import jax
import jax.numpy as jnp
from jax import lax
from jax.experimental import pallas as pl
from jax.experimental.pallas import tpu as pltpu
from jax.sharding import PartitionSpec as P

KSIZE = 5
BF16 = jnp.bfloat16
F32 = jnp.float32


def shift_chan(values, step):
    count = lax.axis_size("chan")
    return lax.ppermute(values, "chan", [(i, (i + step) % count) for i in range(count)])


def swap_seq(values, bit):
    count = lax.axis_size("seq")
    return lax.ppermute(values, "seq", [(i, i ^ bit) for i in range(count)])


def edge_seq(values, step):
    count = lax.axis_size("seq")
    pairs = [(i, i + step) for i in range(count) if 0 <= i + step < count]
    return lax.ppermute(values, "seq", pairs)


def exact_gelu(values):
    return jax.nn.gelu(values, approximate=False)


def in_owner_order(pieces, axis):
    count = len(pieces)
    width = pieces[0].shape[axis]
    joined = jnp.concatenate([pieces[-p % count] for p in range(2 * count)], axis=axis)
    start = (count - lax.axis_index("chan")) * width
    return lax.dynamic_slice_in_dim(joined, start, count * width, axis)


def by_owner(values, axis):
    count = lax.axis_size("chan")
    owner = lax.axis_index("chan")
    width = values.shape[axis] // count
    return [
        lax.dynamic_slice_in_dim(values, (owner + s) % count * width, width, axis)
        for s in range(count)
    ]


def plain_prepare(dna_act, head, tail):
    seq_count, positions, channels = dna_act.shape
    bins = positions // 2
    raw = jnp.concatenate([head, dna_act, tail], axis=1).astype(F32)
    wide = exact_gelu(raw).astype(BF16).astype(F32)
    even = (wide.reshape(seq_count, bins + 2, 2, channels).sum(axis=2) * 0.5).astype(BF16)
    odd = wide[:, 1:-1].reshape(seq_count, bins + 1, 2, channels).sum(axis=2) * 0.5
    odd = odd.astype(BF16)
    windows = jnp.stack(
        [even[:, :bins], odd[:, :bins], even[:, 1:-1], odd[:, 1:], even[:, 2:]]
    )
    slope = jax.vjp(exact_gelu, dna_act.astype(F32))[1](jnp.ones(dna_act.shape, F32))[0]
    return windows, slope


def plain_project(pieces, conv_weight, slabs):
    chosen = in_owner_order(pieces, 1)
    proj = jnp.einsum("kid,md->kim", conv_weight, chosen, preferred_element_type=F32).astype(BF16)
    width = conv_weight.shape[2] // slabs
    slab = lax.axis_index("seq")
    parts = [
        lax.dynamic_slice_in_dim(chosen, (slab ^ t) * width, width, 1) for t in range(slabs)
    ]
    return proj, parts


def plain_partial(windows, projs):
    part = jnp.einsum(
        "ksni,kim->snm", windows, jnp.concatenate(projs, 2), preferred_element_type=F32
    )
    parts = by_owner(part, 1)
    return parts[0], [p.astype(BF16) for p in parts[1:]]


def plain_logit_grad(own, others, counts, mask, group):
    logits = own + sum(o.astype(F32) for o in others)
    block = own.shape[2] // len(group)
    slab = lax.axis_index("seq")
    target = jnp.concatenate(
        [lax.dynamic_slice_in_dim(counts, (slab ^ u) * block, block, 2) for u in group], axis=2
    )
    return (mask[:, :, :1] * (jnp.exp(logits) - target.astype(F32))).astype(BF16)


def plain_outer(windows, pieces, group):
    grads = in_owner_order(pieces, 1)
    outer = jnp.einsum("ksni,snm->kim", windows, grads, preferred_element_type=F32)
    blocks = jnp.split(outer, len(group), axis=2)
    kept = blocks[0::2]
    sent = [b.astype(BF16) for b in blocks[1::2]]
    return grads, kept, sent


def plain_back(grads, projs, edges, slope):
    seq_count, bins, _ = grads[0].shape
    stacked = jnp.concatenate(projs, axis=2)
    block = projs[0].shape[2]
    slab = lax.axis_index("seq")
    slabs = len(projs)

    def reorder(edge, other):
        flip = slab ^ other
        return jnp.concatenate(
            [lax.dynamic_slice_in_dim(edge, (p ^ flip) * block, block, 2) for p in range(slabs)],
            axis=2,
        )

    from_next = reorder(edges[0], jnp.minimum(slab + 1, slabs - 1))
    from_prev = reorder(edges[1], jnp.maximum(slab - 1, 0))
    wide = jnp.concatenate([from_prev, jnp.concatenate(grads, 2), from_next], axis=1)
    back = jnp.einsum("snm,kim->ksni", wide, stacked, preferred_element_type=F32)
    mid, up, down = slice(1, bins + 1), slice(2, bins + 2), slice(0, bins)
    even = back[0][:, up] + back[1][:, mid] + back[2][:, mid] + back[3][:, down] + back[4][:, down]
    odd = back[0][:, up] + back[1][:, up] + back[2][:, mid] + back[3][:, mid] + back[4][:, down]
    grad_acts = jnp.stack([even, odd], axis=2).reshape(slope.shape) * 0.5
    return (grad_acts * slope).astype(BF16)


def plain_tracks(kept, other, conv_weight):
    total = (kept + other.astype(F32)).astype(BF16)
    part = jnp.einsum("kim,kid->md", total, conv_weight, preferred_element_type=F32)
    parts = by_owner(part, 1)
    return total, parts[0], [p.astype(BF16) for p in parts[1:]]


def plain_filters(totals, parts):
    return jnp.einsum(
        "kim,mo->kio",
        jnp.concatenate(totals, 2),
        jnp.concatenate(parts, 0),
        preferred_element_type=F32,
    )


def dot(lhs, rhs, dims=((1,), (0,))):
    return lax.dot_general(lhs, rhs, (dims, ((), ())), preferred_element_type=F32)


def struct(shape, dtype):
    return jax.ShapeDtypeStruct(shape, dtype)


def whole(shape):
    return pl.BlockSpec(shape, lambda *_: (0,) * len(shape))


def lanes(index, width):
    return pl.ds(pl.multiple_of(index * width, 128), width)


def rows_of(index, height):
    return pl.ds(pl.multiple_of(index * height, 16), height)


def call(body, grid, in_specs, out_specs, out_shape, scratch=()):
    return pl.pallas_call(
        body,
        grid_spec=pltpu.PrefetchScalarGridSpec(
            num_scalar_prefetch=1,
            grid=grid,
            in_specs=in_specs,
            out_specs=out_specs,
            scratch_shapes=list(scratch),
        ),
        out_shape=out_shape,
    )


def lane_tiles(channels):
    return [(t, at, min(128, channels - at)) for t, at in enumerate(range(0, channels, 128))]


def here():
    return jnp.stack([lax.axis_index("chan"), lax.axis_index("seq")]).astype(jnp.int32)


def kernel_prepare(dna_act, head, tail):
    seq_count, positions, channels = dna_act.shape
    bins = positions // 2
    tiles = lane_tiles(channels)

    def rounded_gelu(x):
        return (0.5 * x * (1.0 + lax.erf(x * 0.7071067811865476))).astype(BF16).astype(F32)

    def body(where, x_ref, head_ref, tail_ref, win_ref, slope_ref, wide):
        x = x_ref[0].astype(F32)
        cdf = 0.5 * (1.0 + lax.erf(x * 0.7071067811865476))
        slope_ref[0] = cdf + x * jnp.exp(-0.5 * x * x) * 0.3989422804014327
        acts = (x * cdf).astype(BF16).astype(F32)
        first = rounded_gelu(head_ref[0].astype(F32))
        last = rounded_gelu(tail_ref[0].astype(F32))
        for t, at, size in tiles:
            part = slice(at, at + size)
            wide[t, 8 : 8 + positions, :size] = acts[:, part]
            wide[t, 6:8, :size] = first[:, part]
            wide[t, 8 + positions : 10 + positions, :size] = last[:, part]
            reads = [
                wide[t, pl.ds(6 + r, bins, stride=2), :][:, :size] for r in range(KSIZE + 1)
            ]
            for k in range(KSIZE):
                win_ref[k, 0, :, part] = ((reads[k] + reads[k + 1]) * 0.5).astype(BF16)

    return call(
        body,
        (seq_count,),
        [
            pl.BlockSpec((1, positions, channels), lambda s, w: (s, 0, 0)),
            pl.BlockSpec((1, 2, channels), lambda s, w: (s, 0, 0)),
            pl.BlockSpec((1, 2, channels), lambda s, w: (s, 0, 0)),
        ],
        [
            pl.BlockSpec((KSIZE, 1, bins, channels), lambda s, w: (0, s, 0, 0)),
            pl.BlockSpec((1, positions, channels), lambda s, w: (s, 0, 0)),
        ],
        [
            struct((KSIZE, seq_count, bins, channels), BF16),
            struct(dna_act.shape, F32),
        ],
        [pltpu.VMEM((len(tiles), positions + 16, 128), F32)],
    )(here(), dna_act, head, tail)


def kernel_project(pieces, conv_weight, slabs):
    ksize, channels, out_width = conv_weight.shape
    block, cols = pieces[0].shape
    owners = len(pieces)
    width = out_width // slabs

    def body(where, *refs):
        piece_refs, (w_ref, proj_ref), part_refs = (
            refs[:owners], refs[owners : owners + 2], refs[owners + 2 : -1]
        )
        chosen = refs[-1]

        @pl.when(pl.program_id(0) == 0)
        def _():
            for s in range(owners):
                source = lax.rem(where[0] - s + owners, owners)
                chosen[:, lanes(source, cols)] = piece_refs[s][...]
            for t in range(slabs):
                part_refs[t][...] = chosen[:, lanes(where[1] ^ t, width)]

        proj_ref[0] = dot(w_ref[0], chosen[...], ((1,), (1,))).astype(BF16)

    outs = call(
        body,
        (ksize,),
        [whole((block, cols))] * owners
        + [pl.BlockSpec((1, channels, out_width), lambda k, w: (k, 0, 0))],
        [pl.BlockSpec((1, channels, block), lambda k, w: (k, 0, 0))]
        + [whole((block, width))] * slabs,
        [struct((ksize, channels, block), BF16)] + [struct((block, width), BF16)] * slabs,
        [pltpu.VMEM((block, out_width), BF16)],
    )(here(), *pieces, conv_weight)
    return outs[0], outs[1:]


def kernel_partial(windows, projs):
    ksize, seq_count, bins, channels = windows.shape
    owners = lax.axis_size("chan")
    rows = bins // owners
    block = projs[0].shape[2]
    wide = block * len(projs)

    def body(where, win_ref, *refs):
        proj_refs = refs[: len(projs)]
        out_refs, acc = refs[len(projs) : -1], refs[-1]
        total = None
        for k in range(ksize):
            term = dot(win_ref[k, 0], jnp.concatenate([p[k] for p in proj_refs], axis=1))
            total = term if total is None else total + term
        acc[...] = total
        for s in range(owners):
            part = acc[rows_of(lax.rem(where[0] + s, owners), rows)]
            out_refs[s][0] = part.astype(out_refs[s].dtype)

    outs = call(
        body,
        (seq_count,),
        [pl.BlockSpec((ksize, 1, bins, channels), lambda s, w: (0, s, 0, 0))]
        + [whole(projs[0].shape)] * len(projs),
        [pl.BlockSpec((1, rows, wide), lambda s, w: (s, 0, 0))] * owners,
        [struct((seq_count, rows, wide), BF16 if s else F32) for s in range(owners)],
        [pltpu.VMEM((bins, wide), F32)],
    )(here(), windows, *projs)
    return outs[0], outs[1:]


def kernel_logit_grad(own, others, counts, mask, group):
    seq_count, rows, wide = own.shape
    block = wide // len(group)
    inputs = [own, *others]

    def body(where, *refs):
        counts_ref, mask_ref, out_ref = refs[len(inputs) :]
        for s in range(seq_count):
            logits = refs[0][s]
            for other in refs[1 : len(inputs)]:
                logits = logits + other[s].astype(F32)
            target = jnp.concatenate(
                [counts_ref[s, :, lanes(where[1] ^ u, block)] for u in group], axis=1
            )
            mask_wide = jnp.concatenate([mask_ref[s]] * (wide // 128), axis=1)
            out_ref[s] = (mask_wide * (jnp.exp(logits) - target.astype(F32))).astype(BF16)

    arrays = [*inputs, counts, mask]
    return call(
        body, (1,), [whole(a.shape) for a in arrays], whole(own.shape), struct(own.shape, BF16)
    )(here(), *arrays)


def kernel_outer(windows, pieces, group):
    ksize, seq_count, bins, channels = windows.shape
    rows, wide = pieces[0].shape[1:]
    owners = len(pieces)
    block = wide // len(group)

    def body(where, win_ref, *refs):
        piece_refs = refs[:owners]
        grads_ref, kept_ref, sent_ref, grads = refs[owners:]

        @pl.when(pl.program_id(0) == 0)
        def _():
            for s in range(owners):
                source = rows_of(lax.rem(where[0] - s + owners, owners), rows)
                for q in range(seq_count):
                    grads[q, source] = piece_refs[s][q]
            grads_ref[...] = grads[...]

        term = dot(
            win_ref[0].reshape(seq_count * bins, channels),
            grads[...].reshape(seq_count * bins, wide),
            ((0,), (0,)),
        )
        kept_ref[0] = term[:, :block]
        sent_ref[0] = term[:, block:].astype(BF16)

    grads, kept, sent = call(
        body,
        (ksize,),
        [pl.BlockSpec((1, seq_count, bins, channels), lambda k, w: (k, 0, 0, 0))]
        + [whole(pieces[0].shape)] * owners,
        [
            whole((seq_count, bins, wide)),
            pl.BlockSpec((1, channels, block), lambda k, w: (k, 0, 0)),
            pl.BlockSpec((1, channels, block), lambda k, w: (k, 0, 0)),
        ],
        [
            struct((seq_count, bins, wide), BF16),
            struct((ksize, channels, block), F32),
            struct((ksize, channels, block), BF16),
        ],
        [pltpu.VMEM((seq_count, bins, wide), BF16)],
    )(here(), windows, *pieces)
    return grads, [kept], [sent]


def kernel_back(grads, projs, edges, slope):
    seq_count, positions, channels = slope.shape
    bins = positions // 2
    ksize, _, block = projs[0].shape
    slabs = len(projs)
    tiles = lane_tiles(channels)

    def body(where, *refs):
        grad_refs = refs[: len(grads)]
        proj_refs = refs[len(grads) : len(grads) + slabs]
        next_ref, prev_ref, slope_ref, out_ref, shifted, both = refs[len(grads) + slabs :]
        slab = where[1]

        def reorder(ref, other):
            flip = slab ^ other
            row = jnp.concatenate(
                [ref[0, :, lanes(p ^ flip, block)] for p in range(slabs)], axis=1
            )
            return jnp.broadcast_to(row.astype(F32), (16, slabs * block)).astype(BF16)

        from_next = reorder(next_ref, jnp.minimum(slab + 1, slabs - 1))
        from_prev = reorder(prev_ref, jnp.maximum(slab - 1, 0))
        grad = jnp.concatenate([g[0] for g in grad_refs], axis=1)
        stay, moved = [], []
        for k in range(ksize):
            proj = jnp.concatenate([p[k] for p in proj_refs], axis=1)
            back = dot(grad, proj, ((1,), (1,)))
            stay.append(back)
            if k == 2:
                moved.append(None)
                continue
            edge = dot(from_next if k < 2 else from_prev, proj, ((1,), (1,)))[:8]
            shifted[k, 8 : 8 + bins] = back
            if k < 2:
                shifted[k, 8 + bins : 16 + bins] = edge
                moved.append(shifted[k, 9 : 9 + bins])
            else:
                shifted[k, 0:8] = edge
                moved.append(shifted[k, 7 : 7 + bins])
        even = moved[0] + stay[1] + stay[2] + moved[3] + moved[4]
        odd = moved[0] + moved[1] + stay[2] + stay[3] + moved[4]
        for t, at, size in tiles:
            part = slice(at, at + size)
            fill = [jnp.zeros((bins, 128 - size), F32)] if size < 128 else []
            both[t, pl.ds(0, bins, stride=2), :] = jnp.concatenate([even[:, part], *fill], axis=1)
            both[t, pl.ds(1, bins, stride=2), :] = jnp.concatenate([odd[:, part], *fill], axis=1)
            grad_acts = both[t][:, :size]
            out_ref[0, :, part] = (grad_acts * (slope_ref[0, :, part] * 0.5)).astype(BF16)

    wide = grads[0].shape[2]
    edge_spec = pl.BlockSpec((1, 1, slabs * block), lambda s, w: (s, 0, 0))
    long_spec = pl.BlockSpec((1, positions, channels), lambda s, w: (s, 0, 0))
    return call(
        body,
        (seq_count,),
        [pl.BlockSpec((1, bins, wide), lambda s, w: (s, 0, 0))] * len(grads)
        + [whole(projs[0].shape)] * slabs
        + [edge_spec, edge_spec, long_spec],
        long_spec,
        struct(slope.shape, BF16),
        [
            pltpu.VMEM((ksize, bins + 16, channels), F32),
            pltpu.VMEM((len(tiles), positions, 128), F32),
        ],
    )(here(), *grads, *projs, *edges, slope)


def kernel_tracks(kept, other, conv_weight):
    ksize, channels, out_width = conv_weight.shape
    block = kept.shape[2]
    owners = lax.axis_size("chan")
    cols = out_width // owners

    def body(where, kept_ref, other_ref, w_ref, total_ref, *refs):
        out_refs, acc = refs[:-1], refs[-1]
        total = (kept_ref[0] + other_ref[0].astype(F32)).astype(BF16)
        total_ref[0] = total
        term = dot(total, w_ref[0], ((0,), (0,)))

        @pl.when(pl.program_id(0) == 0)
        def _():
            acc[...] = term

        @pl.when(pl.program_id(0) > 0)
        def _():
            acc[...] += term

        @pl.when(pl.program_id(0) == ksize - 1)
        def _():
            for s in range(owners):
                part = acc[:, lanes(lax.rem(where[0] + s, owners), cols)]
                out_refs[s][...] = part.astype(out_refs[s].dtype)

    block_spec = pl.BlockSpec((1, channels, block), lambda k, w: (k, 0, 0))
    outs = call(
        body,
        (ksize,),
        [block_spec, block_spec, pl.BlockSpec((1, channels, out_width), lambda k, w: (k, 0, 0))],
        [block_spec] + [whole((block, cols))] * owners,
        [struct(kept.shape, BF16)]
        + [struct((block, cols), BF16 if s else F32) for s in range(owners)],
        [pltpu.VMEM((block, out_width), F32)],
    )(here(), kept, other, conv_weight)
    return outs[0], outs[1], outs[2:]


def kernel_filters(totals, parts):
    ksize, channels, block = totals[0].shape
    width = parts[0].shape[1]
    count = len(totals)

    def body(where, *refs):
        left = jnp.concatenate([t[0] for t in refs[:count]], axis=1)
        right = jnp.concatenate([p[...] for p in refs[count : 2 * count]], axis=0)
        refs[-1][0] = dot(left, right)

    return call(
        body,
        (ksize,),
        [pl.BlockSpec((1, channels, block), lambda k, w: (k, 0, 0))] * count
        + [whole((block, width))] * count,
        pl.BlockSpec((1, channels, width), lambda k, w: (k, 0, 0)),
        struct((ksize, channels, width), F32),
    )(here(), *totals, *parts)


def local(dna_act, conv_weight, head_weight, track_ids, bin_mask, counts):
    seq_count, positions, channels = dna_act.shape
    out_width = conv_weight.shape[2]
    slabs = lax.axis_size("seq")
    owners = lax.axis_size("chan")
    slab = lax.axis_index("seq")
    block = track_ids.shape[0] // slabs
    cols = head_weight.shape[1]
    rows = bin_mask.shape[1]
    far = slabs // 2

    tiled = (
        slabs == 4
        and block % 128 == 0
        and cols % 128 == 0
        and (out_width // slabs) % 128 == 0
        and rows % 16 == 0
        and positions % 32 == 0
        and channels % 16 == 0
    )
    prepare, project, partial, logit_grad, outer, back, tracks, filters = (
        (kernel_prepare, kernel_project, kernel_partial, kernel_logit_grad, kernel_outer,
         kernel_back, kernel_tracks, kernel_filters)
        if tiled
        else (plain_prepare, plain_project, plain_partial, plain_logit_grad, plain_outer,
              plain_back, plain_tracks, plain_filters)
    )

    my_ids = lax.dynamic_slice_in_dim(track_ids, (slab ^ far) * block, block)
    my_rows = head_weight.at[my_ids].get(mode="promise_in_bounds", wrap_negative_indices=False)
    pieces = [my_rows] + [shift_chan(my_rows, s) for s in range(1, owners)]
    head = edge_seq(dna_act[:, positions - 2 :], 1)
    tail = edge_seq(dna_act[:, :2], -1)
    windows, slope = prepare(dna_act, head, tail)
    proj, parts = project(pieces, conv_weight, slabs)

    slots = {far: proj, 0: swap_seq(proj, far)}
    bit = far // 2
    while bit:
        for u in list(slots):
            slots[u ^ bit] = swap_seq(slots[u], bit)
        bit //= 2
    groups = [[far + u for u in range(far)], list(range(far))]

    mask = jnp.broadcast_to(bin_mask.astype(F32)[:, :, None], (seq_count, rows, 128))
    grads, kept = [], {}
    for group in groups:
        own, sends = partial(windows, [slots[u] for u in group])
        others = [shift_chan(send, s + 1) for s, send in enumerate(sends)]
        mine = logit_grad(own, others, counts, mask, group)
        ring = [mine] + [shift_chan(mine, s) for s in range(1, owners)]
        grad, keeps, sent = outer(windows, ring, group)
        grads.append(grad)
        for n, u in enumerate(group[0::2]):
            kept[u] = keeps[n] + swap_seq(sent[n], 1).astype(F32)

    edges = [
        edge_seq(jnp.concatenate([g[:, :1] for g in grads], axis=2), -1),
        edge_seq(jnp.concatenate([g[:, -1:] for g in grads], axis=2), 1),
    ]
    order = groups[0] + groups[1]
    grad_input = back(grads, [slots[u] for u in order], edges, slope)

    bit = 2
    while bit < far:
        kept = {
            u: kept[u] + swap_seq(kept[u ^ bit].astype(BF16), bit).astype(F32) for u in kept
        }
        bit *= 2
    other = {u ^ far: swap_seq(k.astype(BF16), far) for u, k in kept.items()}
    total, own_tracks, sends = tracks(kept[0], other[0], conv_weight)
    totals = {
        u: total if u == 0 else (kept[u] + other[u].astype(F32)).astype(BF16) for u in kept
    }
    grad_tracks = own_tracks
    for s, send in enumerate(sends):
        grad_tracks = grad_tracks + shift_chan(send, s + 1).astype(F32)
    for u in list(totals):
        totals[u ^ 1] = swap_seq(totals[u], 1)

    parts = [parts[0]] + [swap_seq(parts[t], t) for t in range(1, slabs)]
    grad_conv = filters([totals[u] for u in order], [parts[u ^ far] for u in order])
    return (grad_input, grad_conv, grad_tracks)


def solution(mesh):
    in_specs = (
        P("groups", "seq", "chan"),
        P(None, "chan", None),
        P(None, "chan"),
        P("groups"),
        P("groups", ("seq", "chan")),
        P("groups", ("seq", "chan"), None),
    )
    out_specs = (
        P("groups", "seq", "chan"),
        P("groups", "chan", "seq"),
        P(("groups", "seq"), "chan"),
    )
    return jax.shard_map(local, mesh=mesh, in_specs=in_specs, out_specs=out_specs, check_vma=False)
```

```python
import jax
import jax.numpy as jnp
from jax import lax
from jax.experimental import pallas as pl
from jax.experimental.pallas import tpu as pltpu
from jax.sharding import PartitionSpec as P


KSIZE = 5
BF16 = jnp.bfloat16
F32 = jnp.float32

VMEM_LIMIT = 24 * 1024 * 1024


def shift_chan(values, step):
    count = lax.axis_size("chan")
    return lax.ppermute(values, "chan", [(i, (i + step) % count) for i in range(count)])


def swap_seq(values, bit):
    count = lax.axis_size("seq")
    return lax.ppermute(values, "seq", [(i, i ^ bit) for i in range(count)])


def edge_seq(values, step):
    count = lax.axis_size("seq")
    pairs = [(i, i + step) for i in range(count) if 0 <= i + step < count]
    return lax.ppermute(values, "seq", pairs)


def exact_gelu(values):
    return jax.nn.gelu(values, approximate=False)


def in_owner_order(pieces, axis):
    count = len(pieces)
    width = pieces[0].shape[axis]
    joined = jnp.concatenate([pieces[-p % count] for p in range(2 * count)], axis=axis)
    start = (count - lax.axis_index("chan")) * width
    return lax.dynamic_slice_in_dim(joined, start, count * width, axis)


def by_owner(values, axis):
    count = lax.axis_size("chan")
    owner = lax.axis_index("chan")
    width = values.shape[axis] // count
    return [
        lax.dynamic_slice_in_dim(values, (owner + s) % count * width, width, axis)
        for s in range(count)
    ]


def plain_prepare(dna_act, head, tail, conv_weight):
    seq_count, positions, channels = dna_act.shape
    bins = positions // 2
    raw = jnp.concatenate([head, dna_act, tail], axis=1).astype(F32)
    wide = exact_gelu(raw).astype(BF16).astype(F32)
    even = (wide.reshape(seq_count, bins + 2, 2, channels).sum(axis=2) * 0.5).astype(BF16)
    odd = wide[:, 1:-1].reshape(seq_count, bins + 1, 2, channels).sum(axis=2) * 0.5
    odd = odd.astype(BF16)
    windows = jnp.stack(
        [even[:, :bins], odd[:, :bins], even[:, 1:-1], odd[:, 1:], even[:, 2:]]
    )
    slope = jax.vjp(exact_gelu, dna_act.astype(F32))[1](jnp.ones(dna_act.shape, F32))[0]
    return windows, slope, conv_weight


def plain_project(pieces, conv_weight, slabs, after=None):
    chosen = in_owner_order(pieces, 1)
    proj = jnp.einsum("kid,md->kim", conv_weight, chosen, preferred_element_type=F32).astype(BF16)
    width = conv_weight.shape[2] // slabs
    slab = lax.axis_index("seq")
    parts = [
        lax.dynamic_slice_in_dim(chosen, (slab ^ t) * width, width, 1) for t in range(slabs)
    ]
    return proj, parts


def plain_partial(windows, projs, after=None):
    part = jnp.einsum(
        "ksni,kim->snm", windows, jnp.concatenate(projs, 2), preferred_element_type=F32
    )
    parts = by_owner(part, 1)
    return parts[0], [p.astype(BF16) for p in parts[1:]]


def plain_logit_grad(own, others, counts, mask, group, after=None):
    logits = own + sum(o.astype(F32) for o in others)
    block = own.shape[2] // len(group)
    slab = lax.axis_index("seq")
    target = jnp.concatenate(
        [lax.dynamic_slice_in_dim(counts, (slab ^ u) * block, block, 2) for u in group], axis=2
    )
    return (mask[:, :, :1] * (jnp.exp(logits) - target.astype(F32))).astype(BF16)


def plain_mark(after):
    return after[0]


def plain_turn(windows, parts, after=None):
    return windows, parts


def plain_outer(windows, pieces, group, after=None):
    grads = in_owner_order(pieces, 1)
    outer = jnp.einsum("ksni,snm->kim", windows, grads, preferred_element_type=F32)
    blocks = jnp.split(outer, len(group), axis=2)
    kept = blocks[0::2]
    sent = [b.astype(BF16) for b in blocks[1::2]]
    return grads, (grads[:, :1], grads[:, -1:]), kept, sent


def plain_back(grads, projs, edges, slope, after=None):
    _, bins, _ = grads[0].shape
    stacked = jnp.concatenate(projs, axis=2)
    block = projs[0].shape[2]
    slab = lax.axis_index("seq")
    slabs = len(projs)

    def reorder(edge, other):
        flip = slab ^ other
        return jnp.concatenate(
            [lax.dynamic_slice_in_dim(edge, (p ^ flip) * block, block, 2) for p in range(slabs)],
            axis=2,
        )

    from_next = reorder(edges[0], jnp.minimum(slab + 1, slabs - 1))
    from_prev = reorder(edges[1], jnp.maximum(slab - 1, 0))
    wide = jnp.concatenate([from_prev, jnp.concatenate(grads, 2), from_next], axis=1)
    back = jnp.einsum("snm,kim->ksni", wide, stacked, preferred_element_type=F32)
    mid, up, down = slice(1, bins + 1), slice(2, bins + 2), slice(0, bins)
    even = back[0][:, up] + back[1][:, mid] + back[2][:, mid] + back[3][:, down] + back[4][:, down]
    odd = back[0][:, up] + back[1][:, up] + back[2][:, mid] + back[3][:, mid] + back[4][:, down]
    grad_acts = jnp.stack([even, odd], axis=2).reshape(slope.shape) * 0.5
    return (grad_acts * slope).astype(BF16)


def plain_tracks(kept, other, conv_weight, after=None):
    total = (kept + other.astype(F32)).astype(BF16)
    part = jnp.einsum("kim,kid->md", total, conv_weight, preferred_element_type=F32)
    parts = by_owner(part, 1)
    return total, parts[0], [p.astype(BF16) for p in parts[1:]]


def plain_filters(totals, parts, after=None):
    return jnp.einsum(
        "kim,mo->kio",
        jnp.concatenate(totals, 2),
        jnp.concatenate(parts, 0),
        preferred_element_type=F32,
    )


def dot(lhs, rhs, dims=((1,), (0,))):
    return lax.dot_general(lhs, rhs, (dims, ((), ())), preferred_element_type=F32)


def struct(shape, dtype):
    return jax.ShapeDtypeStruct(shape, dtype)


def vmem(shape, dtype):
    return pltpu.VMEM(shape, dtype)


def lanes(index, width):
    return pl.ds(pl.multiple_of(index * width, 128), width)


def rows_of(index, height):
    return pl.ds(pl.multiple_of(index * height, 16), height)


def call(body, arrays, out_shape, scratch=(), after=None):
    where = jnp.stack([lax.axis_index("chan"), lax.axis_index("seq")]).astype(jnp.int32)
    local_spec = pl.BlockSpec(memory_space=pltpu.VMEM)
    specs = [pl.BlockSpec(memory_space=pltpu.SMEM)] + [local_spec] * len(arrays)
    count = len(arrays) + 1
    extra = list(after or ())
    specs = specs + [pl.BlockSpec(memory_space=pl.ANY)] * len(extra)

    def run(*refs):
        body(*refs[:count], *refs[len(specs) :])

    single = not isinstance(out_shape, (list, tuple))
    return pl.pallas_call(
        run,
        in_specs=specs,
        out_specs=local_spec if single else [local_spec] * len(out_shape),
        out_shape=out_shape,
        scratch_shapes=list(scratch),
        compiler_params=pltpu.CompilerParams(vmem_limit_bytes=VMEM_LIMIT),
    )(where, *arrays, *extra)


def lane_tiles(channels):
    return [(t, at, min(128, channels - at)) for t, at in enumerate(range(0, channels, 128))]


def kernel_prepare(dna_act, head, tail, conv_weight):
    seq_count, positions, channels = dna_act.shape
    bins = positions // 2
    tiles = lane_tiles(channels)

    def rounded_gelu(x):
        return (0.5 * x * (1.0 + lax.erf(x * 0.7071067811865476))).astype(BF16).astype(F32)

    def body(x_ref, head_ref, tail_ref, w_ref, win_ref, slope_ref, held_ref, wide, done):
        fetch = pltpu.make_async_copy(w_ref, held_ref, done)
        fetch.start()
        for q in range(seq_count):
            x = x_ref[q].T.astype(F32)
            cdf = 0.5 * (1.0 + lax.erf(x * 0.7071067811865476))
            slope_ref[q] = cdf + x * jnp.exp(-0.5 * x * x) * 0.3989422804014327
            acts = (x * cdf).astype(BF16).astype(F32)
            first = rounded_gelu(head_ref[q].astype(F32))
            last = rounded_gelu(tail_ref[q].astype(F32))
            for t, at, size in tiles:
                part = slice(at, at + size)
                wide[t, 8 : 8 + positions, :size] = acts[:, part]
                wide[t, 6:8, :size] = first[:, part]
                wide[t, 8 + positions : 10 + positions, :size] = last[:, part]
                reads = [
                    wide[t, pl.ds(6 + r, bins, stride=2), :][:, :size] for r in range(KSIZE + 1)
                ]
                for k in range(KSIZE):
                    win_ref[k, q, :, part] = ((reads[k] + reads[k + 1]) * 0.5).astype(BF16)
        fetch.wait()

    local_spec = pl.BlockSpec(memory_space=pltpu.VMEM)
    return pl.pallas_call(
        body,
        in_specs=[local_spec] * 3 + [pl.BlockSpec(memory_space=pltpu.HBM)],
        out_specs=[local_spec] * 3,
        out_shape=[
            vmem((KSIZE, seq_count, bins, channels), BF16),
            vmem(dna_act.shape, F32),
            vmem(conv_weight.shape, BF16),
        ],
        scratch_shapes=[
            pltpu.VMEM((len(tiles), positions + 16, 128), F32),
            pltpu.SemaphoreType.DMA(()),
        ],
        compiler_params=pltpu.CompilerParams(vmem_limit_bytes=VMEM_LIMIT),
    )(jnp.swapaxes(dna_act, 1, 2), head, tail, conv_weight)


def kernel_project(pieces, conv_weight, slabs, after):
    ksize, channels, out_width = conv_weight.shape
    block, cols = pieces[0].shape
    owners = len(pieces)
    width = out_width // slabs

    def body(where, *refs):
        piece_refs, (w_ref, proj_ref), part_refs = (
            refs[:owners], refs[owners : owners + 2], refs[owners + 2 : -1]
        )
        chosen = refs[-1]
        for s in range(owners):
            source = lax.rem(where[0] - s + owners, owners)
            chosen[:, lanes(source, cols)] = piece_refs[s][...]
        for t in range(slabs):
            part_refs[t][...] = chosen[:, lanes(where[1] ^ t, width)]
        turned = chosen[...].T
        for k in range(ksize):
            proj_ref[k] = dot(w_ref[k], turned).astype(BF16)

    outs = call(
        body,
        [*pieces, conv_weight],
        [struct((ksize, channels, block), BF16)] + [struct((block, width), BF16)] * slabs,
        [pltpu.VMEM((block, out_width), BF16)],
        after,
    )
    return outs[0], outs[1:]


def kernel_partial(windows, projs, after):
    ksize, seq_count, bins, _ = windows.shape
    owners = lax.axis_size("chan")
    rows = bins // owners
    block = projs[0].shape[2]
    wide = block * len(projs)

    def body(where, win_ref, *refs):
        proj_refs = refs[: len(projs)]
        out_refs, acc = refs[len(projs) : -1], refs[-1]
        for q in range(seq_count):
            total = None
            for k in range(ksize):
                term = dot(win_ref[k, q], jnp.concatenate([p[k] for p in proj_refs], axis=1))
                total = term if total is None else total + term
            acc[q] = total
            for s in range(owners):
                part = acc[q, rows_of(lax.rem(where[0] + s, owners), rows)]
                out_refs[s][q] = part.astype(out_refs[s].dtype)

    outs = call(
        body,
        [windows, *projs],
        [vmem((seq_count, rows, wide), F32)]
        + [struct((seq_count, rows, wide), BF16)] * (owners - 1),
        [pltpu.VMEM((seq_count, bins, wide), F32)],
        after,
    )
    return outs[0], outs[1:]


def kernel_mark(after):
    def body(where, out_ref):
        out_ref[...] = jnp.zeros((8, 128), jnp.int32) + where[0]

    return call(body, [], vmem((8, 128), jnp.int32), after=after)


def kernel_turn(windows, parts, after):
    ksize, seq_count, bins, channels = windows.shape

    def body(where, win_ref, *refs):
        out_ref = refs[len(parts)]
        for k in range(ksize):
            for q in range(seq_count):
                out_ref[k, :, q * bins : (q + 1) * bins] = win_ref[k, q].T
        for source, target in zip(refs[: len(parts)], refs[len(parts) + 1 :]):
            target[...] = source[...]

    outs = call(
        body,
        [windows, *parts],
        [vmem((ksize, channels, seq_count * bins), BF16)]
        + [struct(part.shape, BF16) for part in parts],
        after=after,
    )
    return outs[0], outs[1:]


def kernel_logit_grad(own, others, counts, mask, group, after):
    seq_count, _, wide = own.shape
    block = wide // len(group)
    inputs = [own, *others]

    def body(where, *refs):
        counts_ref, mask_ref, out_ref = refs[len(inputs) :]
        for s in range(seq_count):
            logits = refs[0][s]
            for other in refs[1 : len(inputs)]:
                logits = logits + other[s].astype(F32)
            target = jnp.concatenate(
                [counts_ref[s, :, lanes(where[1] ^ u, block)] for u in group], axis=1
            )
            mask_wide = jnp.concatenate([mask_ref[s]] * (wide // 128), axis=1)
            out_ref[s] = (mask_wide * (jnp.exp(logits) - target.astype(F32))).astype(BF16)

    return call(body, [*inputs, counts, mask], struct(own.shape, BF16), after=after)


def kernel_outer(turned, pieces, group, after):
    ksize, channels, length = turned.shape
    seq_count, rows, wide = pieces[0].shape
    owners = len(pieces)
    block = wide // len(group)
    bins = length // seq_count

    def body(where, win_ref, *refs):
        piece_refs = refs[:owners]
        grads_ref, low_ref, high_ref, kept_ref, sent_ref = refs[owners:]
        for s in range(owners):
            source = rows_of(lax.rem(where[0] - s + owners, owners), rows)
            for q in range(seq_count):
                grads_ref[q, source] = piece_refs[s][q]
        for q in range(seq_count):
            low_ref[q] = grads_ref[q, 0:1]
            high_ref[q] = grads_ref[q, bins - 1 : bins]
        grads = grads_ref[...].reshape(length, wide)
        for k in range(ksize):
            term = dot(win_ref[k], grads)
            kept_ref[k] = term[:, :block]
            sent_ref[k] = term[:, block:].astype(BF16)

    grads, low, high, kept, sent = call(
        body,
        [turned, *pieces],
        [
            vmem((seq_count, bins, wide), BF16),
            struct((seq_count, 1, wide), BF16),
            struct((seq_count, 1, wide), BF16),
            vmem((ksize, channels, block), F32),
            struct((ksize, channels, block), BF16),
        ],
        after=after,
    )
    return grads, (low, high), [kept], [sent]


def kernel_back(grads, projs, edges, slope, after):
    seq_count, positions, channels = slope.shape
    bins = positions // 2
    ksize, _, block = projs[0].shape
    slabs = len(projs)
    tiles = lane_tiles(channels)

    def body(where, *refs):
        grad_refs = refs[: len(grads)]
        proj_refs = refs[len(grads) : len(grads) + slabs]
        next_ref, prev_ref, slope_ref, out_ref, shifted, both = refs[len(grads) + slabs :]
        slab = where[1]

        def reorder(ref, q, other):
            flip = slab ^ other
            row = jnp.concatenate(
                [ref[q, :, lanes(p ^ flip, block)] for p in range(slabs)], axis=1
            )
            return jnp.broadcast_to(row.astype(F32), (16, slabs * block)).astype(BF16)

        for q in range(seq_count):
            from_next = reorder(next_ref, q, jnp.minimum(slab + 1, slabs - 1))
            from_prev = reorder(prev_ref, q, jnp.maximum(slab - 1, 0))
            grad = jnp.concatenate([g[q] for g in grad_refs], axis=1)
            stay, moved = [], []
            for k in range(ksize):
                proj = jnp.concatenate([p[k] for p in proj_refs], axis=1)
                back = dot(grad, proj, ((1,), (1,)))
                stay.append(back)
                if k == 2:
                    moved.append(None)
                    continue
                edge = dot(from_next if k < 2 else from_prev, proj, ((1,), (1,)))[:8]
                shifted[k, 8 : 8 + bins] = back
                if k < 2:
                    shifted[k, 8 + bins : 16 + bins] = edge
                    moved.append(shifted[k, 9 : 9 + bins])
                else:
                    shifted[k, 0:8] = edge
                    moved.append(shifted[k, 7 : 7 + bins])
            even = moved[0] + stay[1] + stay[2] + moved[3] + moved[4]
            odd = moved[0] + moved[1] + stay[2] + stay[3] + moved[4]
            for t, at, size in tiles:
                part = slice(at, at + size)
                fill = [jnp.zeros((bins, 128 - size), F32)] if size < 128 else []
                both[t, pl.ds(0, bins, stride=2), :] = jnp.concatenate(
                    [even[:, part], *fill], axis=1
                )
                both[t, pl.ds(1, bins, stride=2), :] = jnp.concatenate(
                    [odd[:, part], *fill], axis=1
                )
                grad_acts = both[t][:, :size]
                out_ref[q, :, part] = (grad_acts * (slope_ref[q, :, part] * 0.5)).astype(BF16)

    return call(
        body,
        [*grads, *projs, *edges, slope],
        struct(slope.shape, BF16),
        [
            pltpu.VMEM((ksize, bins + 16, channels), F32),
            pltpu.VMEM((len(tiles), positions, 128), F32),
        ],
        after,
    )


def kernel_tracks(kept, other, conv_weight, after):
    ksize, _, out_width = conv_weight.shape
    block = kept.shape[2]
    owners = lax.axis_size("chan")
    cols = out_width // owners

    def body(where, kept_ref, other_ref, w_ref, total_ref, *refs):
        out_refs, acc = refs[:-1], refs[-1]
        for k in range(ksize):
            total = (kept_ref[k] + other_ref[k].astype(F32)).astype(BF16)
            total_ref[k] = total
            term = dot(total, w_ref[k], ((0,), (0,)))
            if k:
                acc[...] += term
            else:
                acc[...] = term
        for s in range(owners):
            part = acc[:, lanes(lax.rem(where[0] + s, owners), cols)]
            out_refs[s][...] = part.astype(out_refs[s].dtype)

    outs = call(
        body,
        [kept, other, conv_weight],
        [struct(kept.shape, BF16)]
        + [struct((block, cols), BF16 if s else F32) for s in range(owners)],
        [pltpu.VMEM((block, out_width), F32)],
        after,
    )
    return outs[0], outs[1], outs[2:]


def kernel_filters(totals, parts, after):
    ksize, channels, _ = totals[0].shape
    width = parts[0].shape[1]
    count = len(totals)

    def body(where, *refs):
        right = jnp.concatenate([p[...] for p in refs[count : 2 * count]], axis=0)
        for k in range(ksize):
            left = jnp.concatenate([t[k] for t in refs[:count]], axis=1)
            refs[-1][k] = dot(left, right)

    return call(
        body, [*totals, *parts], struct((ksize, channels, width), F32), after=after
    )


def local(dna_act, conv_weight, head_weight, track_ids, bin_mask, counts):
    seq_count, positions, channels = dna_act.shape
    out_width = conv_weight.shape[2]
    slabs = lax.axis_size("seq")
    owners = lax.axis_size("chan")
    slab = lax.axis_index("seq")
    block = track_ids.shape[0] // slabs
    cols = head_weight.shape[1]
    rows = bin_mask.shape[1]
    far = slabs // 2

    tiled = (
        slabs == 4
        and block % 128 == 0
        and cols % 128 == 0
        and (out_width // slabs) % 128 == 0
        and rows % 16 == 0
        and positions % 32 == 0
        and channels % 16 == 0
    )
    mark, prepare, project, partial, turn, logit_grad, outer, back, tracks, filters = (
        (kernel_mark, kernel_prepare, kernel_project, kernel_partial, kernel_turn, kernel_logit_grad,
         kernel_outer, kernel_back, kernel_tracks, kernel_filters)
        if tiled
        else (plain_mark, plain_prepare, plain_project, plain_partial, plain_turn, plain_logit_grad,
              plain_outer, plain_back, plain_tracks, plain_filters)
    )

    my_ids = lax.dynamic_slice_in_dim(track_ids, (slab ^ far) * block, block)
    my_rows = head_weight.at[my_ids].get(mode="promise_in_bounds", wrap_negative_indices=False)
    pieces = [my_rows] + [shift_chan(my_rows, s) for s in range(1, owners)]
    head = edge_seq(dna_act[:, positions - 2 :], 1)
    tail = edge_seq(dna_act[:, :2], -1)
    windows, slope, conv_weight = prepare(dna_act, head, tail, conv_weight)
    proj, parts = project(pieces, conv_weight, slabs, [slope])

    groups = [[far + u for u in range(far)], list(range(far))]
    slots = {far: proj, 0: swap_seq(proj, far)}

    def spread(first):
        bit = far // 2
        while bit:
            for u in [v for v in slots if v & far == first]:
                slots[u ^ bit] = swap_seq(slots[u], bit)
            bit //= 2

    mask = jnp.broadcast_to(bin_mask.astype(F32)[:, :, None], (seq_count, rows, 128))
    owns, last = [], []
    for name, group in zip("ab", groups):
        if name == "b":
            slots[0], _ = lax.optimization_barrier((slots[0], sends[0]))
        spread(group[0])
        own, sends = partial(windows, [slots[u] for u in group], last)
        owns.append((own, [shift_chan(send, s + 1) for s, send in enumerate(sends)]))
        last = [own]
        if name == "a":
            turned, parts = turn(windows, parts, last)
    parts = [parts[0]] + [swap_seq(parts[t], t) for t in range(1, slabs)]
    rings = []
    for name, group, (own, others) in zip("ab", groups, owns):
        mine = logit_grad(own, others, counts, mask, group, last)
        rings.append([mine] + [shift_chan(mine, s) for s in range(1, owners)])
        last = [mine]
    grads, rims, kept, payload = [], [], {}, {}
    for name, group, ring in zip("ab", groups, rings):
        grad, rim, keeps, sent = outer(turned, ring, group, last)
        grads.append(grad)
        rims.append(rim)
        for n, u in enumerate(group[0::2]):
            received = swap_seq(sent[n], 1)
            kept[u] = keeps[n] + received.astype(F32)
            payload[u] = kept[u].astype(BF16)
        last = [payload[u] for u in group[0::2]]
        if name == "a":
            last = [mark(last)]

    edges = [
        edge_seq(jnp.concatenate([low for low, _ in rims], axis=2), -1),
        edge_seq(jnp.concatenate([high for _, high in rims], axis=2), 1),
    ]
    order = groups[0] + groups[1]

    bit = 2
    while bit < far:
        kept = {u: kept[u] + swap_seq(payload[u ^ bit], bit).astype(F32) for u in kept}
        payload = {u: k.astype(BF16) for u, k in kept.items()}
        bit *= 2
    other = {}
    for u, p in payload.items():
        other[u ^ far] = swap_seq(p, far)
    total, own_tracks, sends = tracks(kept[0], other[0], conv_weight, last)
    grad_input = back(grads, [slots[u] for u in order], edges, slope, [own_tracks])
    totals = {
        u: total if u == 0 else (kept[u] + other[u].astype(F32)).astype(BF16) for u in kept
    }
    grad_tracks = own_tracks
    arrived = [shift_chan(send, s + 1) for s, send in enumerate(sends)]
    for got in arrived:
        grad_tracks = grad_tracks + got.astype(F32)
    for u in list(totals):
        totals[u ^ 1] = swap_seq(totals[u], 1)

    grad_conv = filters(
        [totals[u] for u in order], [parts[u ^ far] for u in order], [grad_input]
    )
    return (grad_input, grad_conv, grad_tracks)


def solution(mesh):
    in_specs = (
        P("groups", "seq", "chan"),
        P(None, "chan", None),
        P(None, "chan"),
        P("groups"),
        P("groups", ("seq", "chan")),
        P("groups", ("seq", "chan"), None),
    )
    out_specs = (
        P("groups", "seq", "chan"),
        P("groups", "chan", "seq"),
        P(("groups", "seq"), "chan"),
    )

    return jax.shard_map(local, mesh=mesh, in_specs=in_specs, out_specs=out_specs, check_vma=False)
```

```python
import jax
import jax.numpy as jnp
from jax import lax
from jax.experimental import pallas as pl
from jax.experimental.pallas import tpu as pltpu
from jax.sharding import PartitionSpec as P


KSIZE = 5
BF16 = jnp.bfloat16
F32 = jnp.float32

VMEM_LIMIT = 24 * 1024 * 1024


def shift_chan(values, step):
    count = lax.axis_size("chan")
    return lax.ppermute(values, "chan", [(i, (i + step) % count) for i in range(count)])


def swap_seq(values, bit):
    count = lax.axis_size("seq")
    return lax.ppermute(values, "seq", [(i, i ^ bit) for i in range(count)])


def edge_seq(values, step):
    count = lax.axis_size("seq")
    pairs = [(i, i + step) for i in range(count) if 0 <= i + step < count]
    return lax.ppermute(values, "seq", pairs)


def exact_gelu(values):
    return jax.nn.gelu(values, approximate=False)


def in_owner_order(pieces, axis):
    count = len(pieces)
    width = pieces[0].shape[axis]
    joined = jnp.concatenate([pieces[-p % count] for p in range(2 * count)], axis=axis)
    start = (count - lax.axis_index("chan")) * width
    return lax.dynamic_slice_in_dim(joined, start, count * width, axis)


def by_owner(values, axis):
    count = lax.axis_size("chan")
    owner = lax.axis_index("chan")
    width = values.shape[axis] // count
    return [
        lax.dynamic_slice_in_dim(values, (owner + s) % count * width, width, axis)
        for s in range(count)
    ]


def plain_prepare(dna_act, conv_weight):
    slope = jax.vjp(exact_gelu, dna_act.astype(F32))[1](jnp.ones(dna_act.shape, F32))[0]
    return dna_act, slope, conv_weight


def plain_patch(dna_act, first, last, head, tail, after=None):
    seq_count, positions, channels = dna_act.shape
    bins = positions // 2
    raw = jnp.concatenate([head, dna_act, tail], axis=1).astype(F32)
    wide = exact_gelu(raw).astype(BF16).astype(F32)
    even = (wide.reshape(seq_count, bins + 2, 2, channels).sum(axis=2) * 0.5).astype(BF16)
    odd = wide[:, 1:-1].reshape(seq_count, bins + 1, 2, channels).sum(axis=2) * 0.5
    odd = odd.astype(BF16)
    return jnp.stack([even[:, :bins], odd[:, :bins], even[:, 1:-1], odd[:, 1:], even[:, 2:]])


def plain_project(pieces, conv_weight, slabs, after=None):
    chosen = in_owner_order(pieces, 1)
    proj = jnp.einsum("kid,md->kim", conv_weight, chosen, preferred_element_type=F32).astype(BF16)
    width = conv_weight.shape[2] // slabs
    slab = lax.axis_index("seq")
    parts = [
        lax.dynamic_slice_in_dim(chosen, (slab ^ t) * width, width, 1) for t in range(slabs)
    ]
    return proj, parts


def plain_partial(windows, projs, after=None):
    part = jnp.einsum(
        "ksni,kim->snm", windows, jnp.concatenate(projs, 2), preferred_element_type=F32
    )
    parts = by_owner(part, 1)
    return parts[0], [p.astype(BF16) for p in parts[1:]]


def plain_logit_grad(own, others, counts, mask, group, after=None):
    logits = own + sum(o.astype(F32) for o in others)
    block = own.shape[2] // len(group)
    slab = lax.axis_index("seq")
    target = jnp.concatenate(
        [lax.dynamic_slice_in_dim(counts, (slab ^ u) * block, block, 2) for u in group], axis=2
    )
    return (mask[:, :, :1] * (jnp.exp(logits) - target.astype(F32))).astype(BF16)


def plain_mark(after):
    return after[0]


def plain_turn(windows, parts, after=None):
    return windows, parts


def plain_outer(windows, pieces, group, after=None):
    grads = in_owner_order(pieces, 1)
    outer = jnp.einsum("ksni,snm->kim", windows, grads, preferred_element_type=F32)
    blocks = jnp.split(outer, len(group), axis=2)
    kept = blocks[0::2]
    sent = [b.astype(BF16) for b in blocks[1::2]]
    return grads, (grads[:, :1], grads[:, -1:]), kept, sent


def plain_back(grads, projs, edges, slope, after=None):
    _, bins, _ = grads[0].shape
    stacked = jnp.concatenate(projs, axis=2)
    block = projs[0].shape[2]
    slab = lax.axis_index("seq")
    slabs = len(projs)

    def reorder(edge, other):
        flip = slab ^ other
        return jnp.concatenate(
            [lax.dynamic_slice_in_dim(edge, (p ^ flip) * block, block, 2) for p in range(slabs)],
            axis=2,
        )

    from_next = reorder(edges[0], jnp.minimum(slab + 1, slabs - 1))
    from_prev = reorder(edges[1], jnp.maximum(slab - 1, 0))
    wide = jnp.concatenate([from_prev, jnp.concatenate(grads, 2), from_next], axis=1)
    back = jnp.einsum("snm,kim->ksni", wide, stacked, preferred_element_type=F32)
    mid, up, down = slice(1, bins + 1), slice(2, bins + 2), slice(0, bins)
    even = back[0][:, up] + back[1][:, mid] + back[2][:, mid] + back[3][:, down] + back[4][:, down]
    odd = back[0][:, up] + back[1][:, up] + back[2][:, mid] + back[3][:, mid] + back[4][:, down]
    grad_acts = jnp.stack([even, odd], axis=2).reshape(slope.shape) * 0.5
    return (grad_acts * slope).astype(BF16)


def plain_tracks(kept, other, conv_weight, after=None):
    total = (kept + other.astype(F32)).astype(BF16)
    part = jnp.einsum("kim,kid->md", total, conv_weight, preferred_element_type=F32)
    parts = by_owner(part, 1)
    return total, parts[0], [p.astype(BF16) for p in parts[1:]]


def plain_filters(totals, parts, shares):
    grad_conv = jnp.einsum(
        "kim,mo->kio",
        jnp.concatenate(totals, 2),
        jnp.concatenate(parts, 0),
        preferred_element_type=F32,
    )
    return grad_conv, sum(share.astype(F32) for share in shares)


def dot(lhs, rhs, dims=((1,), (0,))):
    return lax.dot_general(lhs, rhs, (dims, ((), ())), preferred_element_type=F32)


def struct(shape, dtype):
    return jax.ShapeDtypeStruct(shape, dtype)


def vmem(shape, dtype):
    return pltpu.VMEM(shape, dtype)


def lanes(index, width):
    return pl.ds(pl.multiple_of(index * width, 128), width)


def rows_of(index, height):
    return pl.ds(pl.multiple_of(index * height, 16), height)


def call(body, arrays, out_shape, scratch=(), after=None):
    where = jnp.stack([lax.axis_index("chan"), lax.axis_index("seq")]).astype(jnp.int32)
    local_spec = pl.BlockSpec(memory_space=pltpu.VMEM)
    specs = [pl.BlockSpec(memory_space=pltpu.SMEM)] + [local_spec] * len(arrays)
    count = len(arrays) + 1
    extra = list(after or ())
    specs = specs + [pl.BlockSpec(memory_space=pl.ANY)] * len(extra)

    def run(*refs):
        body(*refs[:count], *refs[len(specs) :])

    single = not isinstance(out_shape, (list, tuple))
    return pl.pallas_call(
        run,
        in_specs=specs,
        out_specs=local_spec if single else [local_spec] * len(out_shape),
        out_shape=out_shape,
        scratch_shapes=list(scratch),
        compiler_params=pltpu.CompilerParams(vmem_limit_bytes=VMEM_LIMIT),
    )(where, *arrays, *extra)


def lane_tiles(channels):
    return [(t, at, min(128, channels - at)) for t, at in enumerate(range(0, channels, 128))]


def kernel_prepare(dna_act, conv_weight):
    seq_count, positions, channels = dna_act.shape
    bins = positions // 2
    tiles = lane_tiles(channels)

    def body(x_ref, w_ref, win_ref, slope_ref, held_ref, wide, done):
        fetch = pltpu.make_async_copy(w_ref, held_ref, done)
        fetch.start()
        for q in range(seq_count):
            x = x_ref[q].T.astype(F32)
            cdf = 0.5 * (1.0 + lax.erf(x * 0.7071067811865476))
            slope_ref[q] = cdf + x * jnp.exp(-0.5 * x * x) * 0.3989422804014327
            acts = (x * cdf).astype(BF16).astype(F32)
            for t, at, size in tiles:
                part = slice(at, at + size)
                wide[t, 8 : 8 + positions, :size] = acts[:, part]
                wide[t, 0:8] = jnp.zeros((8, 128), F32)
                wide[t, 8 + positions : 16 + positions] = jnp.zeros((8, 128), F32)
                reads = [
                    wide[t, pl.ds(6 + r, bins, stride=2), :][:, :size] for r in range(KSIZE + 1)
                ]
                for k in range(KSIZE):
                    win_ref[k, q, :, part] = ((reads[k] + reads[k + 1]) * 0.5).astype(BF16)
        fetch.wait()

    local_spec = pl.BlockSpec(memory_space=pltpu.VMEM)
    return pl.pallas_call(
        body,
        in_specs=[local_spec, pl.BlockSpec(memory_space=pltpu.HBM)],
        out_specs=[local_spec] * 3,
        out_shape=[
            vmem((KSIZE, seq_count, bins, channels), BF16),
            vmem(dna_act.shape, F32),
            vmem(conv_weight.shape, BF16),
        ],
        scratch_shapes=[
            pltpu.VMEM((len(tiles), positions + 16, 128), F32),
            pltpu.SemaphoreType.DMA(()),
        ],
        compiler_params=pltpu.CompilerParams(vmem_limit_bytes=VMEM_LIMIT),
    )(
        jnp.swapaxes(dna_act, 1, 2),
        pltpu.with_memory_space_constraint(conv_weight, pltpu.HBM),
    )


def kernel_patch(windows, first, last, head, tail, after):
    _, seq_count, bins, _ = windows.shape

    def rounded_gelu(ref, q):
        x = ref[q].astype(F32)
        return (0.5 * x * (1.0 + lax.erf(x * 0.7071067811865476))).astype(BF16).astype(F32)

    def body(_, first_ref, last_ref, head_ref, tail_ref, *refs):
        win_ref = refs[-1]

        def put(k, n, one, two):
            win_ref[k, q, n : n + 1] = ((one + two) * 0.5).astype(BF16)

        for q in range(seq_count):
            before = rounded_gelu(head_ref, q)
            behind = rounded_gelu(tail_ref, q)
            put(0, 0, before[0:1], before[1:2])
            put(1, 0, before[1:2], rounded_gelu(first_ref, q)[0:1])
            put(3, bins - 1, rounded_gelu(last_ref, q)[1:2], behind[0:1])
            put(4, bins - 1, behind[0:1], behind[1:2])

    local_spec = pl.BlockSpec(memory_space=pltpu.VMEM)
    return pl.pallas_call(
        body,
        in_specs=[local_spec] * 5 + [pl.BlockSpec(memory_space=pl.ANY)] * len(after),
        out_specs=local_spec,
        out_shape=vmem(windows.shape, BF16),
        input_output_aliases={0: 0},
        compiler_params=pltpu.CompilerParams(vmem_limit_bytes=VMEM_LIMIT),
    )(windows, first, last, head, tail, *after)


def kernel_project(pieces, conv_weight, slabs, after):
    ksize, channels, out_width = conv_weight.shape
    block, cols = pieces[0].shape
    owners = len(pieces)
    width = out_width // slabs

    def body(where, *refs):
        piece_refs, (w_ref, proj_ref), part_refs = (
            refs[:owners], refs[owners : owners + 2], refs[owners + 2 : -1]
        )
        chosen = refs[-1]
        for s in range(owners):
            source = lax.rem(where[0] - s + owners, owners)
            chosen[:, lanes(source, cols)] = piece_refs[s][...]
        for t in range(slabs):
            part_refs[t][...] = chosen[:, lanes(where[1] ^ t, width)]
        turned = chosen[...].T
        for k in range(ksize):
            proj_ref[k] = dot(w_ref[k], turned).astype(BF16)

    outs = call(
        body,
        [*pieces, conv_weight],
        [struct((ksize, channels, block), BF16)] + [struct((block, width), BF16)] * slabs,
        [pltpu.VMEM((block, out_width), BF16)],
        after,
    )
    return outs[0], outs[1:]


def kernel_partial(windows, projs, after):
    ksize, seq_count, bins, _ = windows.shape
    owners = lax.axis_size("chan")
    rows = bins // owners
    block = projs[0].shape[2]
    wide = block * len(projs)

    def body(where, win_ref, *refs):
        proj_refs = refs[: len(projs)]
        out_refs, acc = refs[len(projs) : -1], refs[-1]
        for q in range(seq_count):
            total = None
            for k in range(ksize):
                term = dot(win_ref[k, q], jnp.concatenate([p[k] for p in proj_refs], axis=1))
                total = term if total is None else total + term
            acc[q] = total
            for s in range(owners):
                part = acc[q, rows_of(lax.rem(where[0] + s, owners), rows)]
                out_refs[s][q] = part.astype(out_refs[s].dtype)

    outs = call(
        body,
        [windows, *projs],
        [vmem((seq_count, rows, wide), F32)]
        + [struct((seq_count, rows, wide), BF16)] * (owners - 1),
        [pltpu.VMEM((seq_count, bins, wide), F32)],
        after,
    )
    return outs[0], outs[1:]


def kernel_mark(after):
    def body(where, out_ref):
        out_ref[...] = jnp.zeros((8, 128), jnp.int32) + where[0]

    return call(body, [], vmem((8, 128), jnp.int32), after=after)


def kernel_turn(windows, parts, after):
    ksize, seq_count, bins, channels = windows.shape

    def body(where, win_ref, *refs):
        out_ref = refs[len(parts)]
        for k in range(ksize):
            for q in range(seq_count):
                out_ref[k, :, q * bins : (q + 1) * bins] = win_ref[k, q].T
        for source, target in zip(refs[: len(parts)], refs[len(parts) + 1 :]):
            target[...] = source[...]

    outs = call(
        body,
        [windows, *parts],
        [vmem((ksize, channels, seq_count * bins), BF16)]
        + [struct(part.shape, BF16) for part in parts],
        after=after,
    )
    return outs[0], outs[1:]


def kernel_logit_grad(own, others, counts, mask, group, after):
    seq_count, _, wide = own.shape
    block = wide // len(group)
    inputs = [own, *others]

    def body(where, *refs):
        counts_ref, mask_ref, out_ref = refs[len(inputs) :]
        for s in range(seq_count):
            logits = refs[0][s]
            for other in refs[1 : len(inputs)]:
                logits = logits + other[s].astype(F32)
            target = jnp.concatenate(
                [counts_ref[s, :, lanes(where[1] ^ u, block)] for u in group], axis=1
            )
            mask_wide = jnp.concatenate([mask_ref[s]] * (wide // 128), axis=1)
            out_ref[s] = (mask_wide * (jnp.exp(logits) - target.astype(F32))).astype(BF16)

    return call(body, [*inputs, counts, mask], struct(own.shape, BF16), after=after)


def kernel_outer(turned, pieces, group, after):
    ksize, channels, length = turned.shape
    seq_count, rows, wide = pieces[0].shape
    owners = len(pieces)
    block = wide // len(group)
    bins = length // seq_count

    def body(where, win_ref, *refs):
        piece_refs = refs[:owners]
        grads_ref, low_ref, high_ref, kept_ref, sent_ref = refs[owners:]
        for s in range(owners):
            source = rows_of(lax.rem(where[0] - s + owners, owners), rows)
            for q in range(seq_count):
                grads_ref[q, source] = piece_refs[s][q]
        for q in range(seq_count):
            low_ref[q] = grads_ref[q, 0:1]
            high_ref[q] = grads_ref[q, bins - 1 : bins]
        grads = grads_ref[...].reshape(length, wide)
        for k in range(ksize):
            term = dot(win_ref[k], grads)
            kept_ref[k] = term[:, :block]
            sent_ref[k] = term[:, block:].astype(BF16)

    grads, low, high, kept, sent = call(
        body,
        [turned, *pieces],
        [
            vmem((seq_count, bins, wide), BF16),
            struct((seq_count, 1, wide), BF16),
            struct((seq_count, 1, wide), BF16),
            vmem((ksize, channels, block), F32),
            struct((ksize, channels, block), BF16),
        ],
        after=after,
    )
    return grads, (low, high), [kept], [sent]


def kernel_back(grads, projs, edges, slope, after):
    seq_count, positions, channels = slope.shape
    bins = positions // 2
    ksize, _, block = projs[0].shape
    slabs = len(projs)
    tiles = lane_tiles(channels)

    def body(where, *refs):
        grad_refs = refs[: len(grads)]
        proj_refs = refs[len(grads) : len(grads) + slabs]
        next_ref, prev_ref, slope_ref, out_ref, shifted, both = refs[len(grads) + slabs :]
        slab = where[1]

        def reorder(ref, q, other):
            flip = slab ^ other
            row = jnp.concatenate(
                [ref[q, :, lanes(p ^ flip, block)] for p in range(slabs)], axis=1
            )
            return jnp.broadcast_to(row.astype(F32), (16, slabs * block)).astype(BF16)

        for q in range(seq_count):
            from_next = reorder(next_ref, q, jnp.minimum(slab + 1, slabs - 1))
            from_prev = reorder(prev_ref, q, jnp.maximum(slab - 1, 0))
            grad = jnp.concatenate([g[q] for g in grad_refs], axis=1)
            stay, moved = [], []
            for k in range(ksize):
                proj = jnp.concatenate([p[k] for p in proj_refs], axis=1)
                back = dot(grad, proj, ((1,), (1,)))
                stay.append(back)
                if k == 2:
                    moved.append(None)
                    continue
                edge = dot(from_next if k < 2 else from_prev, proj, ((1,), (1,)))[:8]
                shifted[k, 8 : 8 + bins] = back
                if k < 2:
                    shifted[k, 8 + bins : 16 + bins] = edge
                    moved.append(shifted[k, 9 : 9 + bins])
                else:
                    shifted[k, 0:8] = edge
                    moved.append(shifted[k, 7 : 7 + bins])
            even = moved[0] + stay[1] + stay[2] + moved[3] + moved[4]
            odd = moved[0] + moved[1] + stay[2] + stay[3] + moved[4]
            for t, at, size in tiles:
                part = slice(at, at + size)
                fill = [jnp.zeros((bins, 128 - size), F32)] if size < 128 else []
                both[t, pl.ds(0, bins, stride=2), :] = jnp.concatenate(
                    [even[:, part], *fill], axis=1
                )
                both[t, pl.ds(1, bins, stride=2), :] = jnp.concatenate(
                    [odd[:, part], *fill], axis=1
                )
                grad_acts = both[t][:, :size] * (slope_ref[q, :, part] * 0.5)
                out_ref[q, part] = grad_acts.astype(BF16).T

    turned = call(
        body,
        [*grads, *projs, *edges, slope],
        struct((seq_count, channels, positions), BF16),
        [
            pltpu.VMEM((ksize, bins + 16, channels), F32),
            pltpu.VMEM((len(tiles), positions, 128), F32),
        ],
        after,
    )
    return jnp.swapaxes(turned, 1, 2)


def kernel_tracks(kept, other, conv_weight, after):
    ksize, _, out_width = conv_weight.shape
    block = kept.shape[2]
    owners = lax.axis_size("chan")
    cols = out_width // owners

    def body(where, kept_ref, other_ref, w_ref, total_ref, *refs):
        out_refs, acc = refs[:-1], refs[-1]
        for k in range(ksize):
            total = (kept_ref[k] + other_ref[k].astype(F32)).astype(BF16)
            total_ref[k] = total
            term = dot(total, w_ref[k], ((0,), (0,)))
            if k:
                acc[...] += term
            else:
                acc[...] = term
        for s in range(owners):
            part = acc[:, lanes(lax.rem(where[0] + s, owners), cols)]
            out_refs[s][...] = part.astype(out_refs[s].dtype)

    outs = call(
        body,
        [kept, other, conv_weight],
        [struct(kept.shape, BF16)]
        + [struct((block, cols), BF16 if s else F32) for s in range(owners)],
        [pltpu.VMEM((block, out_width), F32)],
        after,
    )
    return outs[0], outs[1], outs[2:]


def kernel_filters(totals, parts, shares):
    ksize, channels, _ = totals[0].shape
    width = parts[0].shape[1]
    count = len(totals)
    split = [count, 2 * count, 2 * count + len(shares)]

    def body(*refs):
        total_refs, part_refs, share_refs = (
            refs[: split[0]], refs[split[0] : split[1]], refs[split[1] : split[2]]
        )
        conv_ref, tracks_ref, held, done = refs[split[2] :]
        right = jnp.concatenate([p[...] for p in part_refs], axis=0)
        copies = []
        for k in range(ksize):
            left = jnp.concatenate([t[k] for t in total_refs], axis=1)
            held[k] = dot(left, right)
            copies.append(pltpu.make_async_copy(held.at[k], conv_ref.at[k], done.at[k]))
            copies[-1].start()
        tracks = share_refs[0][...]
        for share in share_refs[1:]:
            tracks = tracks + share[...].astype(F32)
        tracks_ref[...] = tracks
        for copy in copies:
            copy.wait()

    local_spec = pl.BlockSpec(memory_space=pltpu.VMEM)
    arrays = [*totals, *parts, *shares]
    return pl.pallas_call(
        body,
        in_specs=[local_spec] * len(arrays),
        out_specs=[pl.BlockSpec(memory_space=pl.ANY), local_spec],
        out_shape=[struct((ksize, channels, width), F32), struct(shares[0].shape, F32)],
        scratch_shapes=[
            pltpu.VMEM((ksize, channels, width), F32),
            pltpu.SemaphoreType.DMA((ksize,)),
        ],
        compiler_params=pltpu.CompilerParams(vmem_limit_bytes=VMEM_LIMIT),
    )(*arrays)


def local(dna_act, conv_weight, head_weight, track_ids, bin_mask, counts):
    seq_count, positions, channels = dna_act.shape
    out_width = conv_weight.shape[2]
    slabs = lax.axis_size("seq")
    owners = lax.axis_size("chan")
    slab = lax.axis_index("seq")
    block = track_ids.shape[0] // slabs
    cols = head_weight.shape[1]
    rows = bin_mask.shape[1]
    far = slabs // 2

    tiled = (
        slabs == 4
        and block % 128 == 0
        and cols % 128 == 0
        and (out_width // slabs) % 128 == 0
        and rows % 16 == 0
        and positions % 32 == 0
        and channels % 16 == 0
    )
    mark, prepare, patch, project, partial, turn, logit_grad, outer, back, tracks, filters = (
        (kernel_mark, kernel_prepare, kernel_patch, kernel_project, kernel_partial, kernel_turn, kernel_logit_grad,
         kernel_outer, kernel_back, kernel_tracks, kernel_filters)
        if tiled
        else (plain_mark, plain_prepare, plain_patch, plain_project, plain_partial, plain_turn, plain_logit_grad,
              plain_outer, plain_back, plain_tracks, plain_filters)
    )

    my_ids = lax.dynamic_slice_in_dim(track_ids, (slab ^ far) * block, block)
    my_rows = head_weight.at[my_ids].get(mode="promise_in_bounds", wrap_negative_indices=False)
    pieces = [my_rows] + [shift_chan(my_rows, s) for s in range(1, owners)]
    first, end = dna_act[:, :2], dna_act[:, positions - 2 :]
    head, tail = edge_seq(end, 1), edge_seq(first, -1)
    windows, slope, conv_weight = prepare(dna_act, conv_weight)
    proj, parts = project(pieces, conv_weight, slabs, [slope])
    windows = patch(windows, first, end, head, tail, [proj])

    groups = [[far + u for u in range(far)], list(range(far))]
    slots = {far: proj, 0: swap_seq(proj, far)}

    def spread(first):
        bit = far // 2
        while bit:
            for u in [v for v in slots if v & far == first]:
                slots[u ^ bit] = swap_seq(slots[u], bit)
            bit //= 2

    mask = jnp.broadcast_to(bin_mask.astype(F32)[:, :, None], (seq_count, rows, 128))
    owns, last = [], []
    for name, group in zip("ab", groups):
        if name == "b":
            slots[0], _ = lax.optimization_barrier((slots[0], sends[0]))
        spread(group[0])
        own, sends = partial(windows, [slots[u] for u in group], last)
        owns.append((own, [shift_chan(send, s + 1) for s, send in enumerate(sends)]))
        last = [own]
        if name == "a":
            turned, parts = turn(windows, parts, last)
    parts = [parts[0]] + [swap_seq(parts[t], t) for t in range(1, slabs)]
    rings = []
    for name, group, (own, others) in zip("ab", groups, owns):
        mine = logit_grad(own, others, counts, mask, group, last)
        rings.append([mine] + [shift_chan(mine, s) for s in range(1, owners)])
        last = [mine]
    grads, rims, kept, payload = [], [], {}, {}
    for name, group, ring in zip("ab", groups, rings):
        grad, rim, keeps, sent = outer(turned, ring, group, last)
        grads.append(grad)
        rims.append(rim)
        for n, u in enumerate(group[0::2]):
            received = swap_seq(sent[n], 1)
            kept[u] = keeps[n] + received.astype(F32)
            payload[u] = kept[u].astype(BF16)
        last = [payload[u] for u in group[0::2]]
        if name == "a":
            last = [mark(last)]

    edges = [
        edge_seq(jnp.concatenate([low for low, _ in rims], axis=2), -1),
        edge_seq(jnp.concatenate([high for _, high in rims], axis=2), 1),
    ]
    order = groups[0] + groups[1]

    bit = 2
    while bit < far:
        kept = {u: kept[u] + swap_seq(payload[u ^ bit], bit).astype(F32) for u in kept}
        payload = {u: k.astype(BF16) for u, k in kept.items()}
        bit *= 2
    other = {}
    for u, p in payload.items():
        other[u ^ far] = swap_seq(p, far)
    grad_input = back(grads, [slots[u] for u in order], edges, slope, last)
    total, own_tracks, sends = tracks(kept[0], other[0], conv_weight, [grad_input])
    totals = {
        u: total if u == 0 else (kept[u] + other[u].astype(F32)).astype(BF16) for u in kept
    }
    arrived = [shift_chan(send, s + 1) for s, send in enumerate(sends)]
    for u in list(totals):
        totals[u ^ 1] = swap_seq(totals[u], 1)

    grad_conv, grad_tracks = filters(
        [totals[u] for u in order], [parts[u ^ far] for u in order], [own_tracks, *arrived]
    )
    return (grad_input, grad_conv, grad_tracks)


def solution(mesh):
    in_specs = (
        P("groups", "seq", "chan"),
        P(None, "chan", None),
        P(None, "chan"),
        P("groups"),
        P("groups", ("seq", "chan")),
        P("groups", ("seq", "chan"), None),
    )
    out_specs = (
        P("groups", "seq", "chan"),
        P("groups", "chan", "seq"),
        P(("groups", "seq"), "chan"),
    )

    return jax.shard_map(local, mesh=mesh, in_specs=in_specs, out_specs=out_specs, check_vma=False)
```

```python
import jax
import jax.numpy as jnp
from jax import lax
from jax.experimental import pallas as pl
from jax.experimental.pallas import tpu as pltpu
from jax.sharding import PartitionSpec as P


KSIZE = 5
BF16 = jnp.bfloat16
F32 = jnp.float32

VMEM_LIMIT = 24 * 1024 * 1024


def shift_chan(values, step):
    count = lax.axis_size("chan")
    return lax.ppermute(values, "chan", [(i, (i + step) % count) for i in range(count)])


def swap_seq(values, bit):
    count = lax.axis_size("seq")
    return lax.ppermute(values, "seq", [(i, i ^ bit) for i in range(count)])


def edge_seq(values, step):
    count = lax.axis_size("seq")
    pairs = [(i, i + step) for i in range(count) if 0 <= i + step < count]
    return lax.ppermute(values, "seq", pairs)


def exact_gelu(values):
    return jax.nn.gelu(values, approximate=False)


def in_owner_order(pieces, axis):
    count = len(pieces)
    width = pieces[0].shape[axis]
    joined = jnp.concatenate([pieces[-p % count] for p in range(2 * count)], axis=axis)
    start = (count - lax.axis_index("chan")) * width
    return lax.dynamic_slice_in_dim(joined, start, count * width, axis)


def by_owner(values, axis):
    count = lax.axis_size("chan")
    owner = lax.axis_index("chan")
    width = values.shape[axis] // count
    return [
        lax.dynamic_slice_in_dim(values, (owner + s) % count * width, width, axis)
        for s in range(count)
    ]


def plain_prepare(dna_act, conv_weight):
    slope = jax.vjp(exact_gelu, dna_act.astype(F32))[1](jnp.ones(dna_act.shape, F32))[0]
    return dna_act, slope, conv_weight


def plain_patch(dna_act, first, last, head, tail, after=None):
    seq_count, positions, channels = dna_act.shape
    bins = positions // 2
    raw = jnp.concatenate([head, dna_act, tail], axis=1).astype(F32)
    wide = exact_gelu(raw).astype(BF16).astype(F32)
    even = (wide.reshape(seq_count, bins + 2, 2, channels).sum(axis=2) * 0.5).astype(BF16)
    odd = wide[:, 1:-1].reshape(seq_count, bins + 1, 2, channels).sum(axis=2) * 0.5
    odd = odd.astype(BF16)
    return jnp.stack([even[:, :bins], odd[:, :bins], even[:, 1:-1], odd[:, 1:], even[:, 2:]])


def plain_project(pieces, conv_weight, slabs, after=None):
    chosen = in_owner_order(pieces, 1)
    proj = jnp.einsum("kid,md->kim", conv_weight, chosen, preferred_element_type=F32).astype(BF16)
    width = conv_weight.shape[2] // slabs
    slab = lax.axis_index("seq")
    parts = [
        lax.dynamic_slice_in_dim(chosen, (slab ^ t) * width, width, 1) for t in range(slabs)
    ]
    return proj, parts


def plain_partial(windows, projs, after=None):
    part = jnp.einsum(
        "ksni,kim->snm", windows, jnp.concatenate(projs, 2), preferred_element_type=F32
    )
    parts = by_owner(part, 1)
    return parts[0], [p.astype(BF16) for p in parts[1:]]


def plain_logit_grad(own, others, counts, mask, group, after=None):
    logits = own + sum(o.astype(F32) for o in others)
    block = own.shape[2] // len(group)
    slab = lax.axis_index("seq")
    target = jnp.concatenate(
        [lax.dynamic_slice_in_dim(counts, (slab ^ u) * block, block, 2) for u in group], axis=2
    )
    return (mask[:, :, :1] * (jnp.exp(logits) - target.astype(F32))).astype(BF16)


def plain_mark(after):
    return after[0]


def plain_turn(windows, parts, after=None):
    return windows, parts


def plain_outer(windows, pieces, group, after=None):
    grads = in_owner_order(pieces, 1)
    outer = jnp.einsum("ksni,snm->kim", windows, grads, preferred_element_type=F32)
    blocks = jnp.split(outer, len(group), axis=2)
    kept = blocks[0::2]
    sent = [b.astype(BF16) for b in blocks[1::2]]
    return grads, (grads[:, :1], grads[:, -1:]), kept, sent


def plain_back(grads, projs, edges, slope, after=None):
    _, bins, _ = grads[0].shape
    stacked = jnp.concatenate(projs, axis=2)
    block = projs[0].shape[2]
    slab = lax.axis_index("seq")
    slabs = len(projs)

    def reorder(edge, other):
        flip = slab ^ other
        return jnp.concatenate(
            [lax.dynamic_slice_in_dim(edge, (p ^ flip) * block, block, 2) for p in range(slabs)],
            axis=2,
        )

    from_next = reorder(edges[0], jnp.minimum(slab + 1, slabs - 1))
    from_prev = reorder(edges[1], jnp.maximum(slab - 1, 0))
    wide = jnp.concatenate([from_prev, jnp.concatenate(grads, 2), from_next], axis=1)
    back = jnp.einsum("snm,kim->ksni", wide, stacked, preferred_element_type=F32)
    mid, up, down = slice(1, bins + 1), slice(2, bins + 2), slice(0, bins)
    even = back[0][:, up] + back[1][:, mid] + back[2][:, mid] + back[3][:, down] + back[4][:, down]
    odd = back[0][:, up] + back[1][:, up] + back[2][:, mid] + back[3][:, mid] + back[4][:, down]
    grad_acts = jnp.stack([even, odd], axis=2).reshape(slope.shape) * 0.5
    return (grad_acts * slope).astype(BF16)


def plain_tracks(kept, other, conv_weight, after=None):
    total = (kept + other.astype(F32)).astype(BF16)
    part = jnp.einsum("kim,kid->md", total, conv_weight, preferred_element_type=F32)
    parts = by_owner(part, 1)
    return total, parts[0], [p.astype(BF16) for p in parts[1:]]


def plain_filters(totals, parts, shares):
    grad_conv = jnp.einsum(
        "kim,mo->kio",
        jnp.concatenate(totals, 2),
        jnp.concatenate(parts, 0),
        preferred_element_type=F32,
    )
    return grad_conv, sum(share.astype(F32) for share in shares)


def dot(lhs, rhs, dims=((1,), (0,))):
    return lax.dot_general(lhs, rhs, (dims, ((), ())), preferred_element_type=F32)


def struct(shape, dtype):
    return jax.ShapeDtypeStruct(shape, dtype)


def vmem(shape, dtype):
    return pltpu.VMEM(shape, dtype)


def lanes(index, width):
    return pl.ds(pl.multiple_of(index * width, 128), width)


def rows_of(index, height):
    return pl.ds(pl.multiple_of(index * height, 16), height)


def call(body, arrays, out_shape, scratch=(), after=None):
    where = jnp.stack([lax.axis_index("chan"), lax.axis_index("seq")]).astype(jnp.int32)
    local_spec = pl.BlockSpec(memory_space=pltpu.VMEM)
    specs = [pl.BlockSpec(memory_space=pltpu.SMEM)] + [local_spec] * len(arrays)
    count = len(arrays) + 1
    extra = list(after or ())
    specs = specs + [pl.BlockSpec(memory_space=pl.ANY)] * len(extra)

    def run(*refs):
        body(*refs[:count], *refs[len(specs) :])

    single = not isinstance(out_shape, (list, tuple))
    return pl.pallas_call(
        run,
        in_specs=specs,
        out_specs=local_spec if single else [local_spec] * len(out_shape),
        out_shape=out_shape,
        scratch_shapes=list(scratch),
        compiler_params=pltpu.CompilerParams(vmem_limit_bytes=VMEM_LIMIT),
    )(where, *arrays, *extra)


def lane_tiles(channels):
    return [(t, at, min(128, channels - at)) for t, at in enumerate(range(0, channels, 128))]


def kernel_prepare(dna_act, conv_weight):
    seq_count, positions, channels = dna_act.shape
    bins = positions // 2
    tiles = lane_tiles(channels)

    def body(x_ref, w_ref, win_ref, slope_ref, held_ref, wide, done):
        fetch = pltpu.make_async_copy(w_ref, held_ref, done)
        fetch.start()
        for q in range(seq_count):
            x = x_ref[q].T.astype(F32)
            cdf = 0.5 * (1.0 + lax.erf(x * 0.7071067811865476))
            slope_ref[q] = cdf + x * jnp.exp(-0.5 * x * x) * 0.3989422804014327
            acts = (x * cdf).astype(BF16).astype(F32)
            for t, at, size in tiles:
                part = slice(at, at + size)
                wide[t, 8 : 8 + positions, :size] = acts[:, part]
                wide[t, 0:8] = jnp.zeros((8, 128), F32)
                wide[t, 8 + positions : 16 + positions] = jnp.zeros((8, 128), F32)
                reads = [
                    wide[t, pl.ds(6 + r, bins, stride=2), :][:, :size] for r in range(KSIZE + 1)
                ]
                for k in range(KSIZE):
                    win_ref[k, q, :, part] = ((reads[k] + reads[k + 1]) * 0.5).astype(BF16)
        fetch.wait()

    local_spec = pl.BlockSpec(memory_space=pltpu.VMEM)
    return pl.pallas_call(
        body,
        in_specs=[local_spec, pl.BlockSpec(memory_space=pltpu.HBM)],
        out_specs=[local_spec] * 3,
        out_shape=[
            vmem((KSIZE, seq_count, bins, channels), BF16),
            vmem(dna_act.shape, F32),
            vmem(conv_weight.shape, BF16),
        ],
        scratch_shapes=[
            pltpu.VMEM((len(tiles), positions + 16, 128), F32),
            pltpu.SemaphoreType.DMA(()),
        ],
        compiler_params=pltpu.CompilerParams(vmem_limit_bytes=VMEM_LIMIT),
    )(
        jnp.swapaxes(dna_act, 1, 2),
        pltpu.with_memory_space_constraint(conv_weight, pltpu.HBM),
    )


def kernel_patch(windows, first, last, head, tail, after):
    _, seq_count, bins, _ = windows.shape

    def rounded_gelu(ref, q):
        x = ref[q].astype(F32)
        return (0.5 * x * (1.0 + lax.erf(x * 0.7071067811865476))).astype(BF16).astype(F32)

    def body(_, first_ref, last_ref, head_ref, tail_ref, *refs):
        win_ref = refs[-1]

        def put(k, n, one, two):
            win_ref[k, q, n : n + 1] = ((one + two) * 0.5).astype(BF16)

        for q in range(seq_count):
            before = rounded_gelu(head_ref, q)
            behind = rounded_gelu(tail_ref, q)
            put(0, 0, before[0:1], before[1:2])
            put(1, 0, before[1:2], rounded_gelu(first_ref, q)[0:1])
            put(3, bins - 1, rounded_gelu(last_ref, q)[1:2], behind[0:1])
            put(4, bins - 1, behind[0:1], behind[1:2])

    local_spec = pl.BlockSpec(memory_space=pltpu.VMEM)
    return pl.pallas_call(
        body,
        in_specs=[local_spec] * 5 + [pl.BlockSpec(memory_space=pl.ANY)] * len(after),
        out_specs=local_spec,
        out_shape=vmem(windows.shape, BF16),
        input_output_aliases={0: 0},
        compiler_params=pltpu.CompilerParams(vmem_limit_bytes=VMEM_LIMIT),
    )(windows, first, last, head, tail, *after)


def kernel_project(pieces, conv_weight, slabs, after):
    ksize, channels, out_width = conv_weight.shape
    block, cols = pieces[0].shape
    owners = len(pieces)
    width = out_width // slabs

    def body(where, *refs):
        piece_refs, (w_ref, proj_ref), part_refs = (
            refs[:owners], refs[owners : owners + 2], refs[owners + 2 : -1]
        )
        chosen = refs[-1]
        for s in range(owners):
            source = lax.rem(where[0] - s + owners, owners)
            chosen[:, lanes(source, cols)] = piece_refs[s][...]
        for t in range(slabs):
            part_refs[t][...] = chosen[:, lanes(where[1] ^ t, width)]
        turned = chosen[...].T
        for k in range(ksize):
            proj_ref[k] = dot(w_ref[k], turned).astype(BF16)

    outs = call(
        body,
        [*pieces, conv_weight],
        [struct((ksize, channels, block), BF16)] + [struct((block, width), BF16)] * slabs,
        [pltpu.VMEM((block, out_width), BF16)],
        after,
    )
    return outs[0], outs[1:]


def kernel_partial(windows, projs, after):
    ksize, seq_count, bins, _ = windows.shape
    owners = lax.axis_size("chan")
    rows = bins // owners
    block = projs[0].shape[2]
    wide = block * len(projs)

    def body(where, win_ref, *refs):
        proj_refs = refs[: len(projs)]
        out_refs, acc = refs[len(projs) : -1], refs[-1]
        for q in range(seq_count):
            total = None
            for k in range(ksize):
                term = dot(win_ref[k, q], jnp.concatenate([p[k] for p in proj_refs], axis=1))
                total = term if total is None else total + term
            acc[q] = total
            for s in range(owners):
                part = acc[q, rows_of(lax.rem(where[0] + s, owners), rows)]
                out_refs[s][q] = part.astype(out_refs[s].dtype)

    outs = call(
        body,
        [windows, *projs],
        [vmem((seq_count, rows, wide), F32)]
        + [struct((seq_count, rows, wide), BF16)] * (owners - 1),
        [pltpu.VMEM((seq_count, bins, wide), F32)],
        after,
    )
    return outs[0], outs[1:]


def kernel_mark(after):
    def body(where, out_ref):
        out_ref[...] = jnp.zeros((8, 128), jnp.int32) + where[0]

    return call(body, [], vmem((8, 128), jnp.int32), after=after)


def kernel_turn(windows, parts, after):
    ksize, seq_count, bins, channels = windows.shape

    def body(where, win_ref, *refs):
        out_ref = refs[len(parts)]
        for k in range(ksize):
            for q in range(seq_count):
                out_ref[k, :, q * bins : (q + 1) * bins] = win_ref[k, q].T
        for source, target in zip(refs[: len(parts)], refs[len(parts) + 1 :]):
            target[...] = source[...]

    outs = call(
        body,
        [windows, *parts],
        [vmem((ksize, channels, seq_count * bins), BF16)]
        + [struct(part.shape, BF16) for part in parts],
        after=after,
    )
    return outs[0], outs[1:]


def kernel_logit_grad(own, others, counts, mask, group, after):
    seq_count, _, wide = own.shape
    block = wide // len(group)
    inputs = [own, *others]

    def body(where, *refs):
        counts_ref, mask_ref, out_ref = refs[len(inputs) :]
        for s in range(seq_count):
            logits = refs[0][s]
            for other in refs[1 : len(inputs)]:
                logits = logits + other[s].astype(F32)
            target = jnp.concatenate(
                [counts_ref[s, :, lanes(where[1] ^ u, block)] for u in group], axis=1
            )
            mask_wide = jnp.concatenate([mask_ref[s]] * (wide // 128), axis=1)
            out_ref[s] = (mask_wide * (jnp.exp(logits) - target.astype(F32))).astype(BF16)

    return call(body, [*inputs, counts, mask], struct(own.shape, BF16), after=after)


def kernel_outer(turned, pieces, group, after):
    ksize, channels, length = turned.shape
    seq_count, rows, wide = pieces[0].shape
    owners = len(pieces)
    block = wide // len(group)
    bins = length // seq_count

    def body(where, win_ref, *refs):
        piece_refs = refs[:owners]
        grads_ref, low_ref, high_ref, kept_ref, sent_ref = refs[owners:]
        for s in range(owners):
            source = rows_of(lax.rem(where[0] - s + owners, owners), rows)
            for q in range(seq_count):
                grads_ref[q, source] = piece_refs[s][q]
        for q in range(seq_count):
            low_ref[q] = grads_ref[q, 0:1]
            high_ref[q] = grads_ref[q, bins - 1 : bins]
        grads = grads_ref[...].reshape(length, wide)
        for k in range(ksize):
            term = dot(win_ref[k], grads)
            kept_ref[k] = term[:, :block]
            sent_ref[k] = term[:, block:].astype(BF16)

    grads, low, high, kept, sent = call(
        body,
        [turned, *pieces],
        [
            vmem((seq_count, bins, wide), BF16),
            struct((seq_count, 1, wide), BF16),
            struct((seq_count, 1, wide), BF16),
            vmem((ksize, channels, block), F32),
            struct((ksize, channels, block), BF16),
        ],
        after=after,
    )
    return grads, (low, high), [kept], [sent]


def kernel_back(grads, projs, edges, slope, after):
    seq_count, positions, channels = slope.shape
    bins = positions // 2
    ksize, _, block = projs[0].shape
    slabs = len(projs)
    tiles = lane_tiles(channels)

    def body(where, *refs):
        grad_refs = refs[: len(grads)]
        proj_refs = refs[len(grads) : len(grads) + slabs]
        next_ref, prev_ref, slope_ref, out_ref, shifted, both = refs[len(grads) + slabs :]
        slab = where[1]

        def reorder(ref, q, other):
            flip = slab ^ other
            row = jnp.concatenate(
                [ref[q, :, lanes(p ^ flip, block)] for p in range(slabs)], axis=1
            )
            return jnp.broadcast_to(row.astype(F32), (16, slabs * block)).astype(BF16)

        for q in range(seq_count):
            from_next = reorder(next_ref, q, jnp.minimum(slab + 1, slabs - 1))
            from_prev = reorder(prev_ref, q, jnp.maximum(slab - 1, 0))
            grad = jnp.concatenate([g[q] for g in grad_refs], axis=1)
            stay, moved = [], []
            for k in range(ksize):
                proj = jnp.concatenate([p[k] for p in proj_refs], axis=1)
                back = dot(grad, proj, ((1,), (1,)))
                stay.append(back)
                if k == 2:
                    moved.append(None)
                    continue
                edge = dot(from_next if k < 2 else from_prev, proj, ((1,), (1,)))[:8]
                shifted[k, 8 : 8 + bins] = back
                if k < 2:
                    shifted[k, 8 + bins : 16 + bins] = edge
                    moved.append(shifted[k, 9 : 9 + bins])
                else:
                    shifted[k, 0:8] = edge
                    moved.append(shifted[k, 7 : 7 + bins])
            even = moved[0] + stay[1] + stay[2] + moved[3] + moved[4]
            odd = moved[0] + moved[1] + stay[2] + stay[3] + moved[4]
            for t, at, size in tiles:
                part = slice(at, at + size)
                fill = [jnp.zeros((bins, 128 - size), F32)] if size < 128 else []
                both[t, pl.ds(0, bins, stride=2), :] = jnp.concatenate(
                    [even[:, part], *fill], axis=1
                )
                both[t, pl.ds(1, bins, stride=2), :] = jnp.concatenate(
                    [odd[:, part], *fill], axis=1
                )
                grad_acts = both[t][:, :size]
                out_ref[q, :, part] = (grad_acts * (slope_ref[q, :, part] * 0.5)).astype(BF16)

    return call(
        body,
        [*grads, *projs, *edges, slope],
        struct(slope.shape, BF16),
        [
            pltpu.VMEM((ksize, bins + 16, channels), F32),
            pltpu.VMEM((len(tiles), positions, 128), F32),
        ],
        after,
    )


def kernel_tracks(kept, other, conv_weight, after):
    ksize, _, out_width = conv_weight.shape
    block = kept.shape[2]
    owners = lax.axis_size("chan")
    cols = out_width // owners

    def body(where, kept_ref, other_ref, w_ref, total_ref, *refs):
        out_refs, acc = refs[:-1], refs[-1]
        for k in range(ksize):
            total = (kept_ref[k] + other_ref[k].astype(F32)).astype(BF16)
            total_ref[k] = total
            term = dot(total, w_ref[k], ((0,), (0,)))
            if k:
                acc[...] += term
            else:
                acc[...] = term
        for s in range(owners):
            part = acc[:, lanes(lax.rem(where[0] + s, owners), cols)]
            out_refs[s][...] = part.astype(out_refs[s].dtype)

    outs = call(
        body,
        [kept, other, conv_weight],
        [struct(kept.shape, BF16)]
        + [struct((block, cols), BF16 if s else F32) for s in range(owners)],
        [pltpu.VMEM((block, out_width), F32)],
        after,
    )
    return outs[0], outs[1], outs[2:]


def kernel_filters(totals, parts, shares):
    ksize, channels, _ = totals[0].shape
    width = parts[0].shape[1]
    count = len(totals)
    split = [count, 2 * count, 2 * count + len(shares)]

    def body(*refs):
        total_refs, part_refs, share_refs = (
            refs[: split[0]], refs[split[0] : split[1]], refs[split[1] : split[2]]
        )
        conv_ref, tracks_ref, held, done = refs[split[2] :]
        right = jnp.concatenate([p[...] for p in part_refs], axis=0)
        copies = []
        for k in range(ksize):
            left = jnp.concatenate([t[k] for t in total_refs], axis=1)
            held[k] = dot(left, right)
            copies.append(pltpu.make_async_copy(held.at[k], conv_ref.at[k], done.at[k]))
            copies[-1].start()
        tracks = share_refs[0][...]
        for share in share_refs[1:]:
            tracks = tracks + share[...].astype(F32)
        tracks_ref[...] = tracks
        for copy in copies:
            copy.wait()

    local_spec = pl.BlockSpec(memory_space=pltpu.VMEM)
    arrays = [*totals, *parts, *shares]
    return pl.pallas_call(
        body,
        in_specs=[local_spec] * len(arrays),
        out_specs=[pl.BlockSpec(memory_space=pl.ANY), local_spec],
        out_shape=[struct((ksize, channels, width), F32), struct(shares[0].shape, F32)],
        scratch_shapes=[
            pltpu.VMEM((ksize, channels, width), F32),
            pltpu.SemaphoreType.DMA((ksize,)),
        ],
        compiler_params=pltpu.CompilerParams(vmem_limit_bytes=VMEM_LIMIT),
    )(*arrays)


def local(dna_act, conv_weight, head_weight, track_ids, bin_mask, counts):
    seq_count, positions, channels = dna_act.shape
    out_width = conv_weight.shape[2]
    slabs = lax.axis_size("seq")
    owners = lax.axis_size("chan")
    slab = lax.axis_index("seq")
    block = track_ids.shape[0] // slabs
    cols = head_weight.shape[1]
    rows = bin_mask.shape[1]
    far = slabs // 2

    tiled = (
        slabs == 4
        and block % 128 == 0
        and cols % 128 == 0
        and (out_width // slabs) % 128 == 0
        and rows % 16 == 0
        and positions % 32 == 0
        and channels % 16 == 0
    )
    mark, prepare, patch, project, partial, turn, logit_grad, outer, back, tracks, filters = (
        (kernel_mark, kernel_prepare, kernel_patch, kernel_project, kernel_partial, kernel_turn, kernel_logit_grad,
         kernel_outer, kernel_back, kernel_tracks, kernel_filters)
        if tiled
        else (plain_mark, plain_prepare, plain_patch, plain_project, plain_partial, plain_turn, plain_logit_grad,
              plain_outer, plain_back, plain_tracks, plain_filters)
    )

    my_ids = lax.dynamic_slice_in_dim(track_ids, (slab ^ far) * block, block)
    my_rows = head_weight.at[my_ids].get(mode="promise_in_bounds", wrap_negative_indices=False)
    pieces = [my_rows] + [shift_chan(my_rows, s) for s in range(1, owners)]
    first, end = dna_act[:, :2], dna_act[:, positions - 2 :]
    head, tail = edge_seq(end, 1), edge_seq(first, -1)
    windows, slope, conv_weight = prepare(dna_act, conv_weight)
    proj, parts = project(pieces, conv_weight, slabs, [slope])
    windows = patch(windows, first, end, head, tail, [proj])

    groups = [[far + u for u in range(far)], list(range(far))]
    slots = {far: proj, 0: swap_seq(proj, far)}

    def spread(first):
        bit = far // 2
        while bit:
            for u in [v for v in slots if v & far == first]:
                slots[u ^ bit] = swap_seq(slots[u], bit)
            bit //= 2

    mask = jnp.broadcast_to(bin_mask.astype(F32)[:, :, None], (seq_count, rows, 128))
    owns, last = [], []
    for name, group in zip("ab", groups):
        if name == "b":
            slots[0], _ = lax.optimization_barrier((slots[0], sends[0]))
        spread(group[0])
        own, sends = partial(windows, [slots[u] for u in group], last)
        owns.append((own, [shift_chan(send, s + 1) for s, send in enumerate(sends)]))
        last = [own]
        if name == "a":
            turned, parts = turn(windows, parts, last)
    parts = [parts[0]] + [swap_seq(parts[t], t) for t in range(1, slabs)]
    rings = []
    for name, group, (own, others) in zip("ab", groups, owns):
        mine = logit_grad(own, others, counts, mask, group, last)
        rings.append([mine] + [shift_chan(mine, s) for s in range(1, owners)])
        last = [mine]
    grads, rims, kept, payload = [], [], {}, {}
    for name, group, ring in zip("ab", groups, rings):
        grad, rim, keeps, sent = outer(turned, ring, group, last)
        grads.append(grad)
        rims.append(rim)
        for n, u in enumerate(group[0::2]):
            received = swap_seq(sent[n], 1)
            kept[u] = keeps[n] + received.astype(F32)
            payload[u] = kept[u].astype(BF16)
        last = [payload[u] for u in group[0::2]]
        if name == "a":
            last = [mark(last)]

    edges = [
        edge_seq(jnp.concatenate([low for low, _ in rims], axis=2), -1),
        edge_seq(jnp.concatenate([high for _, high in rims], axis=2), 1),
    ]
    order = groups[0] + groups[1]

    bit = 2
    while bit < far:
        kept = {u: kept[u] + swap_seq(payload[u ^ bit], bit).astype(F32) for u in kept}
        payload = {u: k.astype(BF16) for u, k in kept.items()}
        bit *= 2
    other = {}
    for u, p in payload.items():
        other[u ^ far] = swap_seq(p, far)
    total, own_tracks, sends = tracks(kept[0], other[0], conv_weight, last)
    grad_input = back(grads, [slots[u] for u in order], edges, slope, [own_tracks])
    totals = {
        u: total if u == 0 else (kept[u] + other[u].astype(F32)).astype(BF16) for u in kept
    }
    arrived = [shift_chan(send, s + 1) for s, send in enumerate(sends)]
    for u in list(totals):
        totals[u ^ 1] = swap_seq(totals[u], 1)

    grad_conv, grad_tracks = filters(
        [totals[u] for u in order], [parts[u ^ far] for u in order], [own_tracks, *arrived]
    )
    return (grad_input, grad_conv, grad_tracks)


def solution(mesh):
    in_specs = (
        P("groups", "seq", "chan"),
        P(None, "chan", None),
        P(None, "chan"),
        P("groups"),
        P("groups", ("seq", "chan")),
        P("groups", ("seq", "chan"), None),
    )
    out_specs = (
        P("groups", "seq", "chan"),
        P("groups", "chan", "seq"),
        P(("groups", "seq"), "chan"),
    )

    return jax.shard_map(local, mesh=mesh, in_specs=in_specs, out_specs=out_specs, check_vma=False)
```
